32 devices in a mesh: replica: 8 (over z, core), shard: 4 (over y, x).
Axes of the slice: x: 2, y: 2, z: 4, core: 2. Of those that a mesh axis runs over, the one named last changes fastest.
Arguments:
- hidden_in: bfloat16 [4, 2048, 2048], P('shard', 'replica'), may hold values from -6 to 6
- piece_index: int32 [4, 2048], P('shard', 'replica'), may hold values from -1 to 7, as said below
- pad_flags: int32 [4, 2048], P('shard', 'replica'), may hold values from 0 to 1, as said below
- cotangent: bfloat16 [4, 2048, 2048], P('shard', 'replica'), may hold values from -6 to 6
- query_weight: bfloat16 [2048, 2048], P('shard'), may hold values from -0.125 to 0.125
- key_weight: bfloat16 [2048, 2048], P('shard'), may hold values from -0.125 to 0.125
- value_weight: bfloat16 [2048, 2048], P('shard'), may hold values from -0.125 to 0.125
- output_weight: bfloat16 [2048, 2048], P('shard'), may hold values from -0.125 to 0.125
- gate_weight: bfloat16 [2048, 8192], P('shard'), may hold values from -0.125 to 0.125
- up_weight: bfloat16 [2048, 8192], P('shard'), may hold values from -0.125 to 0.125
- down_weight: bfloat16 [8192, 2048], P('shard'), may hold values from -0.0625 to 0.0625
- query_gain: bfloat16 [2048], P('shard'), may hold values from 0.25 to 1.75
- key_gain: bfloat16 [2048], P('shard'), may hold values from 0.25 to 1.75
- attention_gain: bfloat16 [2048], P('shard'), may hold values from 0.25 to 1.75
- feed_gain: bfloat16 [2048], P('shard'), may hold values from 0.25 to 1.75
Outputs:
- result: float32 [4, 2048, 2048], P('shard', 'replica')
- grad_hidden: float32 [4, 2048, 2048], P('shard', 'replica')
- grad_query_weight: float32 [2048, 2048], P('shard')
- grad_key_weight: float32 [2048, 2048], P('shard')
- grad_value_weight: float32 [2048, 2048], P('shard')
- grad_output_weight: float32 [2048, 2048], P('shard')
- grad_gate_weight: float32 [2048, 8192], P('shard')
- grad_up_weight: float32 [2048, 8192], P('shard')
- grad_down_weight: float32 [8192, 2048], P('shard')
- grad_query_gain: float32 [2048], P('shard')
- grad_key_gain: float32 [2048], P('shard')
- grad_attention_gain: float32 [2048], P('shard')
- grad_feed_gain: float32 [2048], P('shard')
- stats: float32 [3], replicated
The draws below stay inside these ranges and needn't reach their ends.
Inputs may be any that keep to these rules, and one draw needn't show every extreme that they name: `piece_index`: -1 marks text. A picture piece is an aligned run of 256 tokens of one sequence, all holding that run's index within the sequence; the first run of every sequence is text and the last run of every sequence is a picture piece. `pad_flags`: each sequence ends in a run of one or more padded tokens and has none elsewhere.
All inputs are finite; a program needn't handle non-finite values.
Results may differ from the reference program's by a relative error of at most 0.025.
Values may be sent and summed in bfloat16 or wider, within the bound.
No kernel may reach another device: no remote copies, remote signals or barrier semaphores. Data moves between devices by JAX's collectives and lax.ppermute only.
A program may use at most 576 MiB of HBM per device.

```python
import math
import jax
import jax.numpy as jnp
from jax import lax

D = 2048
HEADS = 16
HEAD = 128
FF = 8192
PIECE = 256
SEQ = 2048
SEQS = 4


def draw_piece_index(key, part):
    blocks = SEQ // PIECE
    chosen = jax.random.randint(jax.random.fold_in(key, 11), (SEQS, blocks), 0, 2)
    block_ids = jnp.arange(blocks, dtype=jnp.int32)
    chosen = chosen * (block_ids > 0).astype(jnp.int32)[None, :]
    chosen = jnp.maximum(chosen, (block_ids == blocks - 1).astype(jnp.int32)[None, :])
    labels = jnp.where(chosen > 0, block_ids[None, :], -1)
    return jnp.repeat(labels, PIECE, axis=1).astype(jnp.int32)


def draw_pad_flags(key, part):
    padded = jax.random.randint(jax.random.fold_in(key, 23), (SEQS, 1), 1, SEQ // 4 + 1)
    places = jnp.arange(SEQ, dtype=jnp.int32)[None, :]
    return (places >= SEQ - padded).astype(jnp.int32)


def block_levels(rng, dims, cuts, low, largest):
    loudness, own = 1.0, jax.random.fold_in(rng, 6)
    for axis_at, blocks in cuts:
        heights = jnp.exp(jax.random.uniform(jax.random.fold_in(own, axis_at), (blocks,), jnp.float32, low / len(cuts), largest / len(cuts)))
        loudness = loudness * jnp.repeat(heights, dims[axis_at] // blocks).reshape([-1 if axis == axis_at else 1 for axis in range(len(dims))])
    return loudness


def noise(stream_key, extent, width, limit, cuts=(), held_as=jnp.bfloat16):
    values = width * jax.random.normal(stream_key, extent, jnp.float32)
    if cuts:
        values = values * block_levels(stream_key, extent, cuts, -0.22, 0.18)
    return jnp.clip(values, -limit, limit).astype(held_as)


def setup_inputs(seed: int = 0) -> dict:
    key_of = jax.random.split(jax.random.key(seed), 16)
    hidden_in = noise(key_of[0], (SEQS, SEQ, D), 1.0, 6.0, ((0, 4), (1, 8)))
    piece_index = draw_piece_index(jax.random.fold_in(key_of[15], 71), 0)
    pad_flags = draw_pad_flags(jax.random.fold_in(key_of[15], 71), 0)
    cotangent = noise(key_of[3], (SEQS, SEQ, D), 1.0, 6.0, ((0, 4), (1, 8)))
    query_weight = noise(key_of[4], (D, D), D ** -0.5, 0.125, ((0, 4),))
    key_weight = noise(key_of[5], (D, D), D ** -0.5, 0.125, ((0, 4),))
    value_weight = noise(key_of[6], (D, D), D ** -0.5, 0.125, ((0, 4),))
    output_weight = noise(key_of[7], (D, D), D ** -0.5, 0.125, ((0, 4),))
    gate_weight = noise(key_of[8], (D, FF), D ** -0.5, 0.125, ((0, 4),))
    up_weight = noise(key_of[9], (D, FF), D ** -0.5, 0.125, ((0, 4),))
    down_weight = noise(key_of[10], (FF, D), FF ** -0.5, 0.0625, ((0, 4),))
    query_gain = jnp.clip(1.0 + 0.15 * jax.random.normal(key_of[11], (D,), jnp.float32), 0.25, 1.75).astype(jnp.bfloat16)
    key_gain = jnp.clip(1.0 + 0.15 * jax.random.normal(key_of[12], (D,), jnp.float32), 0.25, 1.75).astype(jnp.bfloat16)
    attention_gain = jnp.clip(1.0 + 0.15 * jax.random.normal(key_of[13], (D,), jnp.float32), 0.25, 1.75).astype(jnp.bfloat16)
    feed_gain = jnp.clip(1.0 + 0.15 * jax.random.normal(key_of[14], (D,), jnp.float32), 0.25, 1.75).astype(jnp.bfloat16)
    return {"hidden_in": hidden_in, "piece_index": piece_index, "pad_flags": pad_flags, "cotangent": cotangent, "query_weight": query_weight, "key_weight": key_weight, "value_weight": value_weight, "output_weight": output_weight, "gate_weight": gate_weight, "up_weight": up_weight, "down_weight": down_weight, "query_gain": query_gain, "key_gain": key_gain, "attention_gain": attention_gain, "feed_gain": feed_gain}


@jax.custom_vjp
def low(v):
    return lax.optimization_barrier(v.astype(jnp.bfloat16)).astype(jnp.float32)

@jax.custom_vjp
def low_back(v):
    return v

def low_keep(v):
    return (low(v), None)

def low_pass(kept, grad):
    return (grad,)

def back_keep(v):
    return (v, None)

def back_low(kept, grad):
    return (low(grad),)
low.defvjp(low_keep, low_pass)
low_back.defvjp(back_keep, back_low)
epsilon = 1e-06
theta_base = 500000.0
masked_score = -1e+30

def norm_rows(values, gain):
    scaled = values * lax.rsqrt(lax.optimization_barrier(jnp.mean(values * values, axis=-1, keepdims=True)) + epsilon)
    return scaled * gain

def angle_table(positions):
    half_head = HEAD // 2
    rates = theta_base ** (-jnp.arange(half_head).astype(jnp.float32) * (2.0 / HEAD))
    angles = positions.astype(jnp.float32)[:, None] * rates[None, :]
    return (jnp.cos(angles), jnp.sin(angles))

def rotate(values, cosine, sine):
    half_head = HEAD // 2
    first_half = values[..., :half_head]
    second_half = values[..., half_head:]
    cos_wide = cosine[:, None, :]
    sin_wide = sine[:, None, :]
    return jnp.concatenate([first_half * cos_wide - second_half * sin_wide, second_half * cos_wide + first_half * sin_wide], axis=-1)

def product(left, right):
    return jnp.dot(left, right, precision=lax.Precision.HIGHEST)

def layer_pass(hidden_seq, piece_seq, pad_seq, params):
    query_weight, key_weight, value_weight, output_weight, gate_weight, up_weight, down_weight, query_gain, key_gain, attention_gain, feed_gain = params
    seq_len = hidden_seq.shape[0]
    places = jnp.arange(seq_len, dtype=jnp.int32)
    cosine, sine = angle_table(places)
    query_raw = low_back(product(hidden_seq, query_weight))
    key_raw = low_back(product(hidden_seq, key_weight))
    value_low = low(low_back(product(hidden_seq, value_weight))).reshape(seq_len, HEADS, HEAD)
    queries = low(rotate(norm_rows(query_raw, query_gain).reshape(seq_len, HEADS, HEAD), cosine, sine))
    keys = low(rotate(norm_rows(key_raw, key_gain).reshape(seq_len, HEADS, HEAD), cosine, sine))
    block_rows = math.gcd(seq_len, 512)
    score_scale = HEAD ** (-0.5)

    def attend(start):
        query_block = lax.dynamic_slice_in_dim(queries, start, block_rows, 0)
        piece_block = lax.dynamic_slice_in_dim(piece_seq, start, block_rows, 0)
        query_place = start + jnp.arange(block_rows, dtype=jnp.int32)
        scores = jnp.einsum('qhd,khd->hqk', query_block, keys, precision=lax.Precision.HIGHEST) * score_scale
        scores = low_back(scores)
        allowed = (places[None, :] <= query_place[:, None]) | (piece_block[:, None] >= 0) & (piece_block[:, None] == piece_seq[None, :])
        allowed = allowed & (pad_seq[None, :] == 0)
        scores = jnp.where(allowed[None], scores, masked_score)
        highest = lax.optimization_barrier(jnp.max(scores, axis=-1, keepdims=True))
        raised = jnp.exp(scores - highest)
        probs = raised / lax.optimization_barrier(jnp.sum(raised, axis=-1, keepdims=True))
        mixed_block = jnp.einsum('hqk,khd->qhd', low(probs), value_low, precision=lax.Precision.HIGHEST)
        return mixed_block.reshape(block_rows, HEADS * HEAD)
    starts = (jnp.arange(seq_len // block_rows) * block_rows).astype(jnp.int32)
    mixed = lax.map(jax.checkpoint(attend), starts).reshape(seq_len, HEADS * HEAD)
    attended = low(low_back(mixed))
    branch_attn = low_back(product(attended, output_weight))
    residual = hidden_seq + norm_rows(branch_attn, attention_gain)
    residual_low = low(residual)
    gate = low_back(product(residual_low, gate_weight))
    up_values = low_back(product(residual_low, up_weight))
    activated = low(jax.nn.silu(gate) * up_values)
    branch_feed = low_back(product(activated, down_weight))
    result = residual + norm_rows(branch_feed, feed_gain)
    return (result, branch_attn, branch_feed)

def reference(hidden_in, piece_index, pad_flags, cotangent, query_weight, key_weight, value_weight, output_weight, gate_weight, up_weight, down_weight, query_gain, key_gain, attention_gain, feed_gain):
    params = tuple((weight.astype(jnp.float32) for weight in (query_weight, key_weight, value_weight, output_weight, gate_weight, up_weight, down_weight, query_gain, key_gain, attention_gain, feed_gain)))
    inputs = hidden_in.astype(jnp.float32)

    def forward(inputs, params):

        def one_seq(slices):
            return layer_pass(slices[0], slices[1], slices[2], params)
        return lax.map(one_seq, (inputs, piece_index, pad_flags))
    (result, branch_attn, branch_feed), pullback = jax.vjp(forward, inputs, params)
    grad_hidden, grads = pullback((cotangent.astype(jnp.float32), jnp.zeros_like(branch_attn), jnp.zeros_like(branch_feed)))
    valid = (pad_flags == 0).astype(jnp.float32)[..., None]
    counted = jnp.sum(valid) * D
    stats = jnp.stack([jnp.sqrt(jnp.sum(valid * values * values) / counted) for values in (result, branch_attn, branch_feed)])
    return (result, grad_hidden, grads[0], grads[1], grads[2], grads[3], grads[4], grads[5], grads[6], grads[7], grads[8], grads[9], grads[10], stats)
```

```python
import jax
import jax.numpy as jnp
from jax import lax
from jax.experimental import pallas as pl
from jax.experimental.pallas import tpu as pltpu
from jax.sharding import Mesh, PartitionSpec as P

HEADS = 16
HEAD = 128
PIECE = 256

epsilon = 1e-06
theta_base = 500000.0
masked_score = -1e30
score_scale = HEAD ** (-0.5)

BF = jnp.bfloat16
F32 = jnp.float32


def mm(left, right):
    return jnp.dot(left, right, preferred_element_type=F32)


def contract_rows(left, right):
    return lax.dot_general(left, right, (((0,), (0,)), ((), ())), preferred_element_type=F32)


def contract_cols(left, right):
    return lax.dot_general(left, right, (((1,), (1,)), ((), ())), preferred_element_type=F32)


def send_core(values):
    return lax.ppermute(values, "core", [(0, 1), (1, 0)])


def send_shard(values, k):
    count = lax.axis_size("shard")
    return lax.ppermute(values, "shard", [(i, i ^ k) for i in range(count)])


def gather_shard(values):
    count = lax.axis_size("shard")
    if count != 4:
        return [values] + [send_shard(values, k) for k in range(1, count)]
    half = values.shape[0] // 2
    from_x = send_shard(values, 1)
    from_y = send_shard(values, 2)
    far_a = send_shard(from_x[:half], 2)
    far_b = send_shard(from_y[half:], 1)
    return [values, from_x, from_y, jnp.concatenate([far_a, far_b], 0)]


def gather_plane(values):
    mine = gather_shard(values)
    return [mine, [send_core(block) for block in mine]]


def reduce_plane(other, mine):
    count = lax.axis_size("shard")
    total = mine + send_core(other.astype(BF)).astype(F32)
    if count != 4:
        result = total[0]
        for k in range(1, count):
            result = result + send_shard(total[k].astype(BF), k).astype(F32)
        return result
    half = total.shape[1] // 2
    far = total[3].astype(BF)
    via_x = send_shard(far[:half], 1)
    via_y = send_shard(far[half:], 2)
    to_y = jnp.concatenate([total[2][:half] + via_x.astype(F32), total[2][half:]], 0).astype(BF)
    to_x = jnp.concatenate([total[1][:half], total[1][half:] + via_y.astype(F32)], 0).astype(BF)
    return total[0] + send_shard(to_x, 1).astype(F32) + send_shard(to_y, 2).astype(F32)


def sum_plane(values):
    count = lax.axis_size("shard")
    values = values + send_core(values)
    step = 1
    while step < count:
        values = values + send_shard(values, step)
        step *= 2
    return values


def forward_kernel(flags, queries, keys, values, key_bias, mixed, lse):
    rows = queries.shape[0]
    blocks = rows // PIECE
    place_key = lax.broadcasted_iota(jnp.int32, (PIECE, PIECE), 0)
    place_query = lax.broadcasted_iota(jnp.int32, (PIECE, PIECE), 1)
    causal = place_key <= place_query
    for b in range(blocks):
        here = pl.ds(b * PIECE, PIECE)
        whole = flags[b] > 0
        scores = contract_cols(keys[: (b + 1) * PIECE, :], queries[here, :]) * score_scale
        scores = scores + key_bias[: (b + 1) * PIECE, :]
        last = jnp.where(causal | whole, scores[b * PIECE :], masked_score)
        scores = jnp.concatenate([scores[: b * PIECE], last], 0) if b else last
        highest = jnp.max(scores, axis=0, keepdims=True)
        raised = jnp.exp(scores - highest)
        summed = jnp.sum(raised, axis=0, keepdims=True)
        lse[:, here] = highest + jnp.log(summed)
        probs = (raised * (1.0 / summed)).astype(BF)
        mixed[here, :] = contract_rows(probs, values[: (b + 1) * PIECE, :]).astype(mixed.dtype)


def attend_forward(queries, keys, values, key_bias, flags):
    rows, width = queries.shape
    heads = width // HEAD
    column = pl.BlockSpec((rows, HEAD), lambda h, f: (0, h))
    return pl.pallas_call(
        forward_kernel,
        grid_spec=pltpu.PrefetchScalarGridSpec(
            num_scalar_prefetch=1,
            grid=(heads,),
            in_specs=[column, column, column, pl.BlockSpec((rows, 1), lambda h, f: (0, 0))],
            out_specs=[column, pl.BlockSpec((None, 1, rows), lambda h, f: (h, 0, 0))],
        ),
        out_shape=[
            jax.ShapeDtypeStruct((rows, width), BF),
            jax.ShapeDtypeStruct((heads, 1, rows), F32),
        ],
        compiler_params=pltpu.CompilerParams(vmem_limit_bytes=48 * 1024 * 1024),
        name="attend_forward",
    )(flags, queries, keys, values, key_bias)


def backward_kernel(
    flags, queries, keys, values, grad_mixed, key_bias, lse, delta, grad_queries, grad_keys, grad_values, values_acc
):
    rows = queries.shape[0]
    blocks = rows // PIECE
    place_key = lax.broadcasted_iota(jnp.int32, (PIECE, PIECE), 0)
    place_query = lax.broadcasted_iota(jnp.int32, (PIECE, PIECE), 1)
    causal = place_key <= place_query
    grad_keys[...] = jnp.zeros_like(grad_keys)
    values_acc[...] = jnp.zeros_like(values_acc)
    for b in range(blocks):
        here = pl.ds(b * PIECE, PIECE)
        seen = pl.ds(0, (b + 1) * PIECE)
        whole = flags[b] > 0
        query_block = queries[here, :]
        grad_block = grad_mixed[here, :]
        scores = contract_cols(keys[seen, :], query_block) * score_scale + key_bias[seen, :]
        last = jnp.where(causal | whole, scores[b * PIECE :], masked_score)
        scores = jnp.concatenate([scores[: b * PIECE], last], 0) if b else last
        probs = jnp.exp(scores - lse[:, here])
        grad_probs = contract_cols(values[seen, :], grad_block)
        grad_scores = (probs * (grad_probs - delta[:, here])).astype(BF)
        values_acc[seen, :] += mm(probs.astype(BF), grad_block)
        grad_keys[seen, :] += mm(grad_scores, query_block) * score_scale
        grad_queries[here, :] = contract_rows(grad_scores, keys[seen, :]) * score_scale
    grad_values[...] = values_acc[...].astype(grad_values.dtype)


def attend_backward(queries, keys, values, grad_mixed, key_bias, flags, lse, delta):
    rows, width = queries.shape
    heads = width // HEAD
    column = pl.BlockSpec((rows, HEAD), lambda h, f: (0, h))
    line = pl.BlockSpec((None, 1, rows), lambda h, f: (h, 0, 0))
    return pl.pallas_call(
        backward_kernel,
        grid_spec=pltpu.PrefetchScalarGridSpec(
            num_scalar_prefetch=1,
            grid=(heads,),
            in_specs=[column] * 4 + [pl.BlockSpec((rows, 1), lambda h, f: (0, 0)), line, line],
            out_specs=[column] * 3,
            scratch_shapes=[pltpu.VMEM((rows, HEAD), F32)],
        ),
        out_shape=[
            jax.ShapeDtypeStruct((rows, width), F32),
            jax.ShapeDtypeStruct((rows, width), F32),
            jax.ShapeDtypeStruct((rows, width), BF),
        ],
        compiler_params=pltpu.CompilerParams(vmem_limit_bytes=56 * 1024 * 1024),
        name="attend_backward",
    )(flags, queries, keys, values, grad_mixed, key_bias, lse, delta)


def norm_factor(values):
    return lax.rsqrt(jnp.mean(values * values, axis=-1, keepdims=True) + epsilon)


def norm_back(values, factor, gain, cotangent):
    scaled = gain * cotangent
    inner = jnp.mean(values * scaled, axis=-1, keepdims=True)
    grad = factor * scaled - values * (factor * factor * factor) * inner
    return grad, jnp.sum(cotangent * values * factor, axis=0)


def rotate(values, cosine, sine):
    half = HEAD // 2
    first, second = values[..., :half], values[..., half:]
    cos_wide, sin_wide = cosine[:, None, :], sine[:, None, :]
    return jnp.concatenate(
        [first * cos_wide - second * sin_wide, second * cos_wide + first * sin_wide], axis=-1
    )


def rotate_back(values, cosine, sine):
    return rotate(values, cosine, -sine)


def per_device(
    hidden_in,
    piece_index,
    pad_flags,
    cotangent,
    query_weight,
    key_weight,
    value_weight,
    output_weight,
    gate_weight,
    up_weight,
    down_weight,
    query_gain,
    key_gain,
    attention_gain,
    feed_gain,
):
    shards = lax.axis_size("shard")
    planes = lax.axis_size("z")
    shard = lax.axis_index("shard")
    core = lax.axis_index("core")
    plane = lax.axis_index("z")
    tokens = hidden_in[0]
    rows, width = tokens.shape
    chunk = width // shards
    parts = 2 * shards
    head_cols = width // parts
    feed_cols = gate_weight.shape[1] // parts
    seq_len = rows * 2 * planes
    everything = 2 * rows * shards

    def swap_cores(values):
        return jnp.where(core == 0, values, values[::-1])

    def plane_relative(values):
        return jnp.stack(
            [
                lax.dynamic_index_in_dim(values, (shard ^ k) * 2 + (core ^ r), 0, keepdims=False)
                for r in range(2)
                for k in range(shards)
            ]
        )

    def plane_absolute(values):
        return jnp.stack(
            [
                lax.dynamic_index_in_dim(values, (core ^ r) * shards + (shard ^ j), 0, keepdims=False)
                for j in range(shards)
                for r in range(2)
            ]
        )

    by_chunk = tokens.reshape(rows, shards, chunk).transpose(1, 0, 2)
    by_seq = lax.all_to_all(by_chunk, "shard", 0, 0, tiled=True)
    mine = lax.all_to_all(by_seq, "z", 0, 0, tiled=True).reshape(planes * rows, chunk)

    def column_block(weight, k, cols):
        return lax.dynamic_slice_in_dim(weight, ((shard ^ k) * 2 + core) * cols, cols, 1)

    def input_block(k):
        return jnp.concatenate(
            [column_block(w, k, head_cols) for w in (query_weight, key_weight, value_weight)], 1
        )

    def feed_block(k):
        return jnp.concatenate([column_block(w, k, feed_cols) for w in (gate_weight, up_weight)], 1)

    input_blocks = [input_block(0)] + [send_shard(input_block(k), k) for k in range(1, shards)]
    whole_input = jnp.concatenate(input_blocks, 0)
    feed_blocks = [feed_block(0)] + [send_shard(feed_block(k), k) for k in range(1, shards)]
    whole_feed = jnp.zeros((width, 2 * feed_cols), BF)
    for k in range(shards):
        whole_feed = lax.dynamic_update_slice_in_dim(whole_feed, feed_blocks[k], (shard ^ k) * chunk, 0)
    out_block = lax.dynamic_slice_in_dim(output_weight, core * head_cols, head_cols, 0)
    down_block = lax.dynamic_slice_in_dim(down_weight, core * feed_cols, feed_cols, 0)
    gains = lax.all_gather(jnp.stack([attention_gain, feed_gain]), "shard", axis=1, tiled=True).astype(F32)
    query_gain_here = lax.dynamic_slice_in_dim(query_gain, core * head_cols, head_cols, 0).astype(F32)
    key_gain_here = lax.dynamic_slice_in_dim(key_gain, core * head_cols, head_cols, 0).astype(F32)
    info = jnp.stack([piece_index[0], pad_flags[0]]).astype(BF)
    info_all = lax.all_gather(info, ("z", "core", "shard"), axis=0)
    info_all = info_all.reshape(planes, 2, shards, 2, rows)
    info_seq = lax.dynamic_index_in_dim(info_all, plane, 2, keepdims=False).astype(F32)
    piece_seq = info_seq[:, :, 0].reshape(seq_len)
    pad_seq = info_seq[:, :, 1].reshape(seq_len)
    block_flags = (piece_seq.reshape(-1, PIECE)[:, 0] >= 0.0).astype(jnp.int32)
    key_bias = jnp.where(pad_seq > 0.0, masked_score, 0.0)[:, None]

    gathered = gather_plane(mine)
    inputs_here = jnp.concatenate([jnp.concatenate(blocks, 1) for blocks in gathered], 0)
    raw = mm(inputs_here, whole_input).reshape(2, planes, rows, 3 * head_cols)
    raw = swap_cores(raw).transpose(1, 0, 2, 3).reshape(seq_len, 3 * head_cols)
    query_raw = raw[:, :head_cols]
    key_raw = raw[:, head_cols : 2 * head_cols]
    value_low = raw[:, 2 * head_cols :].astype(BF)
    squares = sum_plane(
        jnp.stack([jnp.sum(query_raw * query_raw, -1), jnp.sum(key_raw * key_raw, -1)])
    )
    factors = lax.rsqrt(squares / width + epsilon)
    query_factor, key_factor = factors[0][:, None], factors[1][:, None]
    rates = theta_base ** (-jnp.arange(HEAD // 2).astype(F32) * (2.0 / HEAD))
    angles = jnp.arange(seq_len, dtype=jnp.int32).astype(F32)[:, None] * rates[None, :]
    cosine, sine = jnp.cos(angles), jnp.sin(angles)
    heads_here = head_cols // HEAD

    def turn(values, factor, gain):
        normed = (values * factor * gain).reshape(seq_len, heads_here, HEAD)
        return rotate(normed, cosine, sine).reshape(seq_len, head_cols).astype(BF)

    query_low = turn(query_raw, query_factor, query_gain_here)
    key_low = turn(key_raw, key_factor, key_gain_here)
    attended_seq, lse = attend_forward(query_low, key_low, value_low, key_bias, block_flags)

    attended = lax.all_to_all(
        attended_seq.reshape(planes, 2 * rows, head_cols), "z", 0, 0, tiled=True
    ).reshape(parts, rows, head_cols)
    attended = plane_relative(attended).reshape(everything, head_cols)
    half = everything // 2

    def blocks_of(values):
        return values.reshape(shards, rows, values.shape[-1])

    branch_attn = reduce_plane(
        blocks_of(mm(attended[half:], out_block)), blocks_of(mm(attended[:half], out_block))
    )
    attn_factor = norm_factor(branch_attn)
    residual = tokens.astype(F32) + branch_attn * attn_factor * gains[0]
    gathered = gather_plane(residual.astype(BF))
    residual_all = jnp.concatenate(gathered[0] + gathered[1], 0)
    gate = mm(residual_all, whole_feed[:, :feed_cols])
    up = mm(residual_all, whole_feed[:, feed_cols:])
    activated = (jax.nn.silu(gate) * up).astype(BF)
    branch_feed = reduce_plane(
        blocks_of(mm(activated[half:], down_block)), blocks_of(mm(activated[:half], down_block))
    )
    feed_factor = norm_factor(branch_feed)
    result = residual + branch_feed * feed_factor * gains[1]

    grad_out = cotangent[0].astype(F32)
    grad_feed, grad_feed_gain = norm_back(branch_feed, feed_factor, gains[1], grad_out)
    gathered = gather_plane(grad_feed.astype(BF))
    grad_feed_all = jnp.concatenate(gathered[0] + gathered[1], 0)
    grad_act = contract_cols(grad_feed_all, down_block)
    grad_down = contract_rows(activated, grad_feed_all).astype(BF)
    down_part = lax.psum_scatter(grad_down, "z", scatter_dimension=0, tiled=True)
    sigmoid = jax.nn.sigmoid(gate)
    grad_gate = (grad_act * up * sigmoid * (1.0 + gate * (1.0 - sigmoid))).astype(BF)
    grad_up = (grad_act * gate * sigmoid).astype(BF)
    grad_both = jnp.concatenate([grad_gate, grad_up], 1)
    grad_feed_in = reduce_plane(
        blocks_of(contract_cols(grad_both[half:], whole_feed)),
        blocks_of(contract_cols(grad_both[:half], whole_feed)),
    )

    def scatter_rows(term):
        cols = term.shape[1]
        term = term.astype(BF).reshape(shards, planes, chunk // planes, cols).transpose(1, 0, 2, 3)
        part = lax.psum_scatter(term.reshape(width, cols), "z", scatter_dimension=0, tiled=True)
        return part.reshape(shards, chunk // planes, cols)

    feed_part = scatter_rows(contract_rows(residual_all, grad_both))

    grad_resid = grad_out + grad_feed_in
    grad_branch, grad_attention_gain = norm_back(branch_attn, attn_factor, gains[0], grad_resid)
    gathered = gather_plane(grad_branch.astype(BF))
    grad_branch_all = jnp.concatenate(gathered[0] + gathered[1], 0)
    grad_mixed = contract_cols(grad_branch_all, out_block).astype(BF)
    grad_output = contract_rows(attended, grad_branch_all).astype(BF)
    grad_mixed = plane_absolute(grad_mixed.reshape(parts, rows, head_cols))
    grad_mixed = lax.all_to_all(
        grad_mixed.reshape(shards, 2 * rows, head_cols), "z", 0, 0, tiled=True
    ).reshape(seq_len, head_cols)
    delta = jnp.sum(
        (grad_mixed.astype(F32) * attended_seq.astype(F32)).reshape(seq_len, heads_here, HEAD), -1
    ).T.reshape(heads_here, 1, seq_len)
    grad_queries, grad_keys, grad_values = attend_backward(
        query_low, key_low, value_low, grad_mixed, key_bias, block_flags, lse, delta
    )

    def turn_back(grad, values, factor, gain):
        turned = rotate_back(grad.reshape(seq_len, heads_here, HEAD), cosine, sine)
        turned = turned.reshape(seq_len, head_cols)
        scaled = turned * gain
        return scaled, jnp.sum(values * scaled, -1), jnp.sum(turned * values * factor, 0)

    query_scaled, query_inner, grad_query_gain = turn_back(
        grad_queries, query_raw, query_factor, query_gain_here
    )
    key_scaled, key_inner, grad_key_gain = turn_back(grad_keys, key_raw, key_factor, key_gain_here)
    inner = sum_plane(jnp.stack([query_inner, key_inner])) / width

    def finish(scaled, values, factor, inner_row):
        return (factor * scaled - values * (factor * factor * factor) * inner_row[:, None]).astype(BF)

    grad_raw = jnp.concatenate(
        [
            finish(query_scaled, query_raw, query_factor, inner[0]),
            finish(key_scaled, key_raw, key_factor, inner[1]),
            grad_values,
        ],
        1,
    )
    grad_raw = grad_raw.reshape(planes, 2, rows, 3 * head_cols).transpose(1, 0, 2, 3)
    grad_raw = swap_cores(grad_raw).reshape(seq_len, 3 * head_cols)
    seq_half = seq_len // 2

    def chunks_of(values):
        return jnp.stack([contract_cols(values, block) for block in input_blocks])

    grad_chunk = reduce_plane(chunks_of(grad_raw[seq_half:]), chunks_of(grad_raw[:seq_half]))
    grad_chunk = grad_chunk.astype(BF).reshape(planes, rows, chunk)
    grad_chunk = lax.all_to_all(grad_chunk, "z", 0, 0, tiled=True)
    grad_chunk = lax.all_to_all(grad_chunk, "shard", 0, 0, tiled=True)
    grad_tokens = grad_resid + grad_chunk.transpose(1, 0, 2).reshape(rows, width).astype(F32)

    input_part = scatter_rows(contract_rows(inputs_here, grad_raw))
    output_part = lax.psum_scatter(grad_output, "z", scatter_dimension=0, tiled=True)

    def to_owner(part, is_relative):
        blocks = []
        for k in range(shards):
            block = part[k] if is_relative else lax.dynamic_index_in_dim(part, shard ^ k, 0, keepdims=False)
            blocks.append(send_shard(block, k) if k else block)
        stacked = jnp.stack(blocks)
        return jnp.stack(
            [lax.dynamic_index_in_dim(stacked, shard ^ j, 0, keepdims=False) for j in range(shards)]
        )

    def copies(values):
        return lax.all_gather(values, ("z", "core"), axis=0).reshape((planes, 2) + values.shape)

    down_all = copies(down_part)
    grad_down_weight = down_all.transpose(1, 0, 2, 3).reshape(down_weight.shape).astype(F32)
    feed_all = copies(to_owner(feed_part, False))

    def wide(values, weight):
        return values.transpose(0, 3, 2, 1, 4).reshape(weight.shape).astype(F32)

    grad_gate_weight = wide(feed_all[..., :feed_cols], gate_weight)
    grad_up_weight = wide(feed_all[..., feed_cols:], up_weight)
    output_all = copies(output_part)
    grad_output_weight = output_all.transpose(1, 0, 2, 3).reshape(output_weight.shape).astype(F32)
    input_all = copies(to_owner(input_part, True))
    grad_inputs = [
        wide(input_all[..., i * head_cols : (i + 1) * head_cols], query_weight) for i in range(3)
    ]

    valid = (pad_flags[0] == 0).astype(F32)[:, None]
    stat_terms = jnp.stack(
        [
            jnp.sum(valid * result * result),
            jnp.sum(valid * branch_attn * branch_attn),
            jnp.sum(valid * branch_feed * branch_feed),
            jnp.sum(valid),
        ]
    )
    place = (shard * 2 + core) * head_cols
    blank = jnp.zeros((2, width), F32)
    gain_heads = lax.dynamic_update_slice(
        blank, jnp.stack([grad_query_gain, grad_key_gain]), (jnp.int32(0), place)
    )
    terms = jnp.concatenate(
        [
            gain_heads.reshape(-1),
            grad_attention_gain,
            grad_feed_gain,
            stat_terms,
        ]
    )
    terms = lax.psum(terms, ("z", "core", "shard"))
    gain_terms = terms[: 4 * width].reshape(4, width)
    gain_width = query_gain.shape[0]
    gain_mine = lax.dynamic_slice_in_dim(gain_terms, shard * gain_width, gain_width, 1)
    stat_terms = terms[4 * width :]
    stats = jnp.sqrt(stat_terms[:3] / (stat_terms[3] * width))
    return (
        result[None],
        grad_tokens[None],
        grad_inputs[0],
        grad_inputs[1],
        grad_inputs[2],
        grad_output_weight,
        grad_gate_weight,
        grad_up_weight,
        grad_down_weight,
        gain_mine[0],
        gain_mine[1],
        gain_mine[2],
        gain_mine[3],
        stats,
    )


def solution(mesh):
    devices = mesh.devices.reshape(mesh.shape["replica"] // 2, 2, mesh.shape["shard"])
    split = Mesh(devices, ("z", "core", "shard"))
    tokens = ("z", "core")
    placed = (
        (P("shard", tokens, None), P("shard", tokens), P("shard", tokens), P("shard", tokens, None))
        + (P("shard", None),) * 7
        + (P("shard"),) * 4
    )
    return jax.shard_map(
        per_device,
        mesh=split,
        in_specs=placed,
        out_specs=(P("shard", tokens, None),) * 2
        + (P("shard", None),) * 7
        + (P("shard"),) * 4
        + (P(),),
        check_vma=False,
    )
```

```python
import functools

import jax
import jax.numpy as jnp
from jax import lax
from jax.experimental import pallas as pl
from jax.experimental.pallas import tpu as pltpu
from jax.sharding import Mesh, PartitionSpec as P

HEADS = 16
HEAD = 128
PIECE = 256

epsilon = 1e-06
theta_base = 500000.0
masked_score = -1e30
score_scale = HEAD ** (-0.5)

BF = jnp.bfloat16
F32 = jnp.float32


def mm(left, right):
    return jnp.dot(left, right, preferred_element_type=F32)


def contract_rows(left, right):
    return lax.dot_general(left, right, (((0,), (0,)), ((), ())), preferred_element_type=F32)


def contract_cols(left, right):
    return lax.dot_general(left, right, (((1,), (1,)), ((), ())), preferred_element_type=F32)


def send_core(values):
    return lax.ppermute(values, "core", [(0, 1), (1, 0)])


def send_shard(values, k):
    count = lax.axis_size("shard")
    return lax.ppermute(values, "shard", [(i, i ^ k) for i in range(count)])


def send_plane(values, k):
    count = lax.axis_size("z")
    return lax.ppermute(values, "z", [(i, i ^ k) for i in range(count)])


def gather_shard(values):
    count = lax.axis_size("shard")
    if count != 4:
        return [values] + [send_shard(values, k) for k in range(1, count)]
    half = values.shape[0] // 2
    from_x = send_shard(values, 1)
    from_y = send_shard(values, 2)
    far_a = send_shard(from_x[:half], 2)
    far_b = send_shard(from_y[half:], 1)
    return [values, from_x, from_y, jnp.concatenate([far_a, far_b], 0)]


def gather_plane(values):
    mine = gather_shard(values)
    return [mine, [send_core(block) for block in mine]]


def reduce_shard(term):
    count = lax.axis_size("shard")
    everything = slice(None)
    if count != 4:
        result = term(0, everything)
        for k in range(1, count):
            result = result + send_shard(term(k, everything).astype(BF), k).astype(F32)
        return result
    near, far = slice(0, term.rows // 2), slice(term.rows // 2, None)
    via_x = send_shard(term(3, near).astype(BF), 1)
    via_y = send_shard(term(3, far).astype(BF), 2)
    to_y = jnp.concatenate([(term(2, near) + via_x.astype(F32)).astype(BF), term(2, far).astype(BF)], 0)
    to_x = jnp.concatenate([term(1, near).astype(BF), (term(1, far) + via_y.astype(F32)).astype(BF)], 0)
    return term(0, everything) + send_shard(to_x, 1).astype(F32) + send_shard(to_y, 2).astype(F32)


def reduce_plane(other, mine):
    got = send_core(other.astype(BF))
    mine, got = lax.optimization_barrier((mine.astype(BF), got))

    def term(k, part):
        return mine[k, part].astype(F32) + got[k, part].astype(F32)

    term.rows = mine.shape[1]
    return reduce_shard(term)


def sum_over_planes(values):
    count = lax.axis_size("z")
    step = 1
    while step < count:
        values = values + lax.ppermute(values, "z", [(i, i ^ step) for i in range(count)])
        step *= 2
    return values


def sum_plane(values, swapped=False):
    count = lax.axis_size("shard")
    other = send_core(values)
    values = values + (other[:, ::-1] if swapped else other)
    step = 1
    while step < count:
        values = values + send_shard(values, step)
        step *= 2
    return values


def terms_kernel(tokens, grads, out):
    total = contract_rows(tokens[...], grads[...]).astype(BF)
    out[...] = total.reshape(out.shape)


def weight_terms(tokens, grads, shards, planes):
    rows, width = tokens.shape
    cols = grads.shape[1]
    chunk = width // shards
    return pl.pallas_call(
        terms_kernel,
        grid=(shards,),
        in_specs=[
            pl.BlockSpec((rows, chunk), lambda i: (0, i)),
            pl.BlockSpec((rows, cols), lambda i: (0, 0), pipeline_mode=pl.Buffered(1)),
        ],
        out_specs=pl.BlockSpec((planes, 1, chunk // planes, cols), lambda i: (0, i, 0, 0)),
        out_shape=jax.ShapeDtypeStruct((planes, shards, chunk // planes, cols), BF),
        compiler_params=pltpu.CompilerParams(vmem_limit_bytes=40 * 1024 * 1024),
        name="weight_terms",
    )(tokens, grads)


def columns_kernel(copies, *outs):
    _, cores, shards, rows, cols = copies.shape
    share = cols // len(outs)
    for n, out in enumerate(outs):
        for s in range(shards):
            for c in range(cores):
                at = (s * cores + c) * share
                out[:, at : at + share] = copies[0, c, s, :, n * share : (n + 1) * share].astype(F32)


def columns_out(copies, count):
    planes, cores, shards, rows, cols = copies.shape
    wide = shards * cores * cols // count
    return pl.pallas_call(
        columns_kernel,
        grid=(planes,),
        in_specs=[pl.BlockSpec((1,) + copies.shape[1:], lambda i: (i, 0, 0, 0, 0))],
        out_specs=[pl.BlockSpec((rows, wide), lambda i: (i, 0))] * count,
        out_shape=[jax.ShapeDtypeStruct((planes * rows, wide), F32)] * count,
        compiler_params=pltpu.CompilerParams(vmem_limit_bytes=40 * 1024 * 1024),
        name="columns_out",
    )(copies)


def rows_kernel(copies, out):
    out[...] = copies[0, 0].astype(F32)


def rows_out(copies):
    planes, cores, rows, cols = copies.shape
    return pl.pallas_call(
        rows_kernel,
        grid=(planes, cores),
        in_specs=[pl.BlockSpec((1, 1, rows, cols), lambda i, j: (i, j, 0, 0))],
        out_specs=pl.BlockSpec((rows, cols), lambda i, j: (j * planes + i, 0)),
        out_shape=jax.ShapeDtypeStruct((planes * cores * rows, cols), F32),
        name="rows_out",
    )(copies)


def project_kernel(count, *refs):
    tokens, weights, raw, squares = refs[: 2 * count], refs[2 * count : 3 * count], refs[-2], refs[-1]
    chunk = tokens[0].shape[1]
    third = raw.shape[1] // 3
    block = pl.program_id(0) * pl.num_programs(1) + pl.program_id(1)
    for r in range(2):

        @pl.when(pl.program_id(0) == r)
        def _():
            total = mm(tokens[r * count][...], weights[0][:chunk, :])
            for k in range(1, count):
                total += mm(tokens[r * count + k][...], weights[k][:chunk, :])
            raw[...] = total
            for n in range(2):
                squared = total[:, n * third : (n + 1) * third]
                squared = squared * squared
                folded = squared[:, :HEAD]
                for h in range(1, third // HEAD):
                    folded += squared[:, h * HEAD : (h + 1) * HEAD]
                squares[n, pl.ds(block, 1), :] = as_row(folded)


def project(pieces, weights):
    count = len(weights)
    rows, chunk = pieces[0][0].shape
    cols = weights[0].shape[1]
    steps = rows // PIECE

    def spec(r):
        return pl.BlockSpec((PIECE, chunk), lambda a, i: (jnp.where(a == r, i, (steps - 1) * (a > r)), 0))

    return pl.pallas_call(
        functools.partial(project_kernel, count),
        grid=(2, steps),
        in_specs=[spec(r) for r in range(2) for _ in range(count)]
        + [pl.BlockSpec(w.shape, lambda a, i: (0, 0), pipeline_mode=pl.Buffered(1)) for w in weights],
        out_specs=[
            pl.BlockSpec((PIECE, cols), lambda a, i: (a * steps + i, 0)),
            pl.BlockSpec((2, 2 * steps, PIECE), lambda a, i: (0, 0, 0)),
        ],
        out_shape=[
            jax.ShapeDtypeStruct((2 * rows, cols), F32),
            jax.ShapeDtypeStruct((2, 2 * steps, PIECE), F32),
        ],
        compiler_params=pltpu.CompilerParams(vmem_limit_bytes=40 * 1024 * 1024),
        name="project",
    )(*pieces[0], *pieces[1], *weights)


def input_terms_kernel(count, *refs):
    tokens, grads, out = refs[: 2 * count], refs[2 * count], refs[2 * count + 1]
    rows = tokens[0].shape[0]
    planes, _, share, cols = out.shape
    for k in range(count):
        total = contract_rows(tokens[k][...], grads[:rows, :]) + contract_rows(tokens[count + k][...], grads[rows:, :])
        out[:, k] = total.astype(BF).reshape(planes, share, cols)


def input_terms(pieces, grads, planes):
    count = len(pieces[0])
    chunk = pieces[0][0].shape[1]
    return pl.pallas_call(
        functools.partial(input_terms_kernel, count),
        out_shape=jax.ShapeDtypeStruct((planes, count, chunk // planes, grads.shape[1]), BF),
        compiler_params=pltpu.CompilerParams(vmem_limit_bytes=56 * 1024 * 1024),
        name="input_terms",
    )(*pieces[0], *pieces[1], grads)


def memory_block(block, where, blocks, per_device):
    core, here = where
    plane, rest = divmod(block, 2 * per_device)
    which, inside = divmod(rest, per_device)
    return (which ^ core) * (blocks // 2) + (plane ^ here) * per_device + inside


def as_columns(row):
    return jnp.broadcast_to(row, (HEAD, PIECE)).T


def as_row(values):
    return jnp.sum(values.T, axis=0, keepdims=True)


def factor_of(squares):
    return lax.rsqrt(squares * (1.0 / (HEADS * HEAD)) + epsilon)


def forward_kernel(
    per_device, flags, raw_q, raw_k, raw_v, squares, gain_q, gain_k, cosine, sine, key_bias,
    mixed, queries, keys, values, lse,
):
    rows = queries.shape[0]
    blocks = rows // PIECE
    core = (flags[blocks], flags[blocks + 1])
    place_key = lax.broadcasted_iota(jnp.int32, (PIECE, PIECE), 0)
    place_query = lax.broadcasted_iota(jnp.int32, (PIECE, PIECE), 1)
    causal = place_key <= place_query
    for b in range(blocks):
        here = pl.ds(b * PIECE, PIECE)
        from_block = memory_block(b, core, blocks, per_device)
        there = pl.ds(pl.multiple_of(from_block * PIECE, PIECE), PIECE)
        for n, (raw, gain, turned) in enumerate(((raw_q, gain_q, queries), (raw_k, gain_k, keys))):
            factor = as_columns(factor_of(squares[n, pl.ds(from_block, 1), :]))
            normed = raw[there, :] * factor * gain[...]
            turned[here, :] = (
                normed * cosine[here, :] + pltpu.roll(normed, HEAD // 2, 1) * sine[here, :]
            ).astype(BF)
        values[here, :] = raw_v[there, :].astype(BF)
    for b in range(blocks):
        here = pl.ds(b * PIECE, PIECE)
        seen = pl.ds(0, (b + 1) * PIECE)
        whole = flags[b] > 0
        scores = contract_cols(keys[seen, :], queries[here, :]) * score_scale + key_bias[seen, :]
        last = jnp.where(causal | whole, scores[b * PIECE :], masked_score)
        scores = jnp.concatenate([scores[: b * PIECE], last], 0) if b else last
        highest = jnp.max(scores, axis=0, keepdims=True)
        raised = jnp.exp(scores - highest)
        summed = jnp.sum(raised, axis=0, keepdims=True)
        lse[:, here] = highest + jnp.log(summed)
        probs = (raised * (1.0 / summed)).astype(BF)
        mixed[here, :] = contract_rows(probs, values[seen, :]).astype(mixed.dtype)


def attend_forward(raw, squares, gain_q, gain_k, cosine, sine, key_bias, flags, per_device):
    rows = raw.shape[0]
    heads = raw.shape[1] // (3 * HEAD)
    blocks = rows // PIECE
    column = pl.BlockSpec((rows, HEAD), lambda h, f: (0, h))
    table = pl.BlockSpec((rows, HEAD), lambda h, f: (0, 0), pipeline_mode=pl.Buffered(1))
    gain = pl.BlockSpec((1, HEAD), lambda h, f: (0, h))
    turned = jax.ShapeDtypeStruct((rows, heads * HEAD), BF)
    return pl.pallas_call(
        functools.partial(forward_kernel, per_device),
        grid_spec=pltpu.PrefetchScalarGridSpec(
            num_scalar_prefetch=1,
            grid=(heads,),
            in_specs=[
                column,
                pl.BlockSpec((rows, HEAD), lambda h, f: (0, heads + h)),
                pl.BlockSpec((rows, HEAD), lambda h, f: (0, 2 * heads + h)),
                pl.BlockSpec((2, blocks, PIECE), lambda h, f: (0, 0, 0)),
                gain,
                gain,
                table,
                table,
                pl.BlockSpec((rows, 1), lambda h, f: (0, 0), pipeline_mode=pl.Buffered(1)),
            ],
            out_specs=[column] * 4 + [pl.BlockSpec((None, 1, rows), lambda h, f: (h, 0, 0))],
        ),
        out_shape=[turned] * 4 + [jax.ShapeDtypeStruct((heads, 1, rows), F32)],
        compiler_params=pltpu.CompilerParams(vmem_limit_bytes=52 * 1024 * 1024),
        name="attend_forward",
    )(flags, raw, raw, raw, squares, gain_q, gain_k, cosine, sine, key_bias)


def backward_kernel(
    per_device, flags, queries, keys, values, grad_mixed, mixed, raw_q, raw_k, squares, gain_q, gain_k,
    cosine, sine, key_bias, lse,
    scaled_q, scaled_k, grad_values, inner, grad_gains, keys_acc, values_acc,
):
    rows = queries.shape[0]
    blocks = rows // PIECE
    core = (flags[blocks], flags[blocks + 1])
    place_key = lax.broadcasted_iota(jnp.int32, (PIECE, PIECE), 0)
    place_query = lax.broadcasted_iota(jnp.int32, (PIECE, PIECE), 1)
    causal = place_key <= place_query
    keys_acc[...] = jnp.zeros_like(keys_acc)
    values_acc[...] = jnp.zeros_like(values_acc)
    grad_gains[...] = jnp.zeros_like(grad_gains)

    def turn_back(n, b, grad, raw, gain, scaled_out):
        here = pl.ds(b * PIECE, PIECE)
        block = memory_block(b, core, blocks, per_device)
        there = pl.ds(pl.multiple_of(block * PIECE, PIECE), PIECE)
        turned = grad * cosine[here, :] - pltpu.roll(grad, HEAD // 2, 1) * sine[here, :]
        raw_block = raw[there, :]
        scaled = turned * gain[...]
        scaled_out[there, :] = scaled
        inner[n, pl.ds(block, 1), :] = as_row(raw_block * scaled)
        factor = as_columns(factor_of(squares[n, pl.ds(block, 1), :]))
        grad_gains[n : n + 1, :] += jnp.sum(turned * raw_block * factor, axis=0, keepdims=True)

    for b in range(blocks):
        here = pl.ds(b * PIECE, PIECE)
        whole = flags[b] > 0
        query_block = queries[here, :]
        grad_block = grad_mixed[here, :]
        delta = as_row(grad_block.astype(F32) * mixed[here, :].astype(F32))
        grad_query = jnp.zeros((PIECE, HEAD), F32)
        for first in range(0, b + 1, 8):
            last = min(first + 8, b + 1)
            seen = pl.ds(first * PIECE, (last - first) * PIECE)
            scores = contract_cols(keys[seen, :], query_block) * score_scale + key_bias[seen, :]
            if last == b + 1:
                edge = (b - first) * PIECE
                final = jnp.where(causal | whole, scores[edge:], masked_score)
                scores = jnp.concatenate([scores[:edge], final], 0) if edge else final
            probs = jnp.exp(scores - lse[:, here])
            grad_probs = contract_cols(values[seen, :], grad_block)
            grad_scores = (probs * (grad_probs - delta)).astype(BF)
            values_acc[seen, :] += mm(probs.astype(BF), grad_block)
            keys_acc[seen, :] += mm(grad_scores, query_block)
            grad_query += contract_rows(grad_scores, keys[seen, :])
        turn_back(0, b, grad_query * score_scale, raw_q, gain_q, scaled_q)
    for b in range(blocks):
        here = pl.ds(b * PIECE, PIECE)
        turn_back(1, b, keys_acc[here, :] * score_scale, raw_k, gain_k, scaled_k)
        block = memory_block(b, core, blocks, per_device)
        there = pl.ds(pl.multiple_of(block * PIECE, PIECE), PIECE)
        grad_values[there, :] = values_acc[here, :].astype(BF)


def attend_backward(
    queries, keys, values, grad_mixed, mixed, raw, squares, gain_q, gain_k, cosine, sine, key_bias, flags, lse,
    per_device,
):
    rows, width = queries.shape
    heads = width // HEAD
    blocks = rows // PIECE
    column = pl.BlockSpec((rows, HEAD), lambda h, f: (0, h))
    table = pl.BlockSpec((rows, HEAD), lambda h, f: (0, 0), pipeline_mode=pl.Buffered(1))
    gain = pl.BlockSpec((1, HEAD), lambda h, f: (0, h))
    return pl.pallas_call(
        functools.partial(backward_kernel, per_device),
        grid_spec=pltpu.PrefetchScalarGridSpec(
            num_scalar_prefetch=1,
            grid=(heads,),
            in_specs=[column] * 5
            + [
                column,
                pl.BlockSpec((rows, HEAD), lambda h, f: (0, heads + h)),
                pl.BlockSpec((2, blocks, PIECE), lambda h, f: (0, 0, 0)),
                gain,
                gain,
                table,
                table,
                pl.BlockSpec((rows, 1), lambda h, f: (0, 0), pipeline_mode=pl.Buffered(1)),
                pl.BlockSpec((None, 1, rows), lambda h, f: (h, 0, 0)),
            ],
            out_specs=[column] * 3
            + [
                pl.BlockSpec((None, 2, blocks, PIECE), lambda h, f: (h, 0, 0, 0)),
                pl.BlockSpec((None, 2, HEAD), lambda h, f: (h, 0, 0)),
            ],
            scratch_shapes=[pltpu.VMEM((rows, HEAD), F32)] * 2,
        ),
        out_shape=[
            jax.ShapeDtypeStruct((rows, width), F32),
            jax.ShapeDtypeStruct((rows, width), F32),
            jax.ShapeDtypeStruct((rows, width), BF),
            jax.ShapeDtypeStruct((heads, 2, blocks, PIECE), F32),
            jax.ShapeDtypeStruct((heads, 2, HEAD), F32),
        ],
        compiler_params=pltpu.CompilerParams(vmem_limit_bytes=56 * 1024 * 1024),
        name="attend_backward",
    )(
        flags, queries, keys, values, grad_mixed, mixed, raw, raw, squares, gain_q, gain_k, cosine, sine,
        key_bias, lse,
    )


def finish_kernel(scaled_q, scaled_k, grad_values, raw, squares, inner, out):
    block = pl.program_id(0)
    width = scaled_q.shape[1]
    for n, scaled in enumerate((scaled_q, scaled_k)):
        factor_row = factor_of(squares[n, pl.ds(block, 1), :])
        inner_row = inner[n, pl.ds(block, 1), :] * (1.0 / (HEADS * HEAD))
        factor = as_columns(factor_row)
        slope = as_columns(factor_row * factor_row * factor_row * inner_row)
        for h in range(width // HEAD):
            at = n * width + h * HEAD
            out[:, at : at + HEAD] = (
                factor * scaled[:, h * HEAD : (h + 1) * HEAD] - raw[:, at : at + HEAD] * slope
            ).astype(BF)
    out[:, 2 * width :] = grad_values[...]


def finish(scaled_q, scaled_k, grad_values, raw, squares, inner):
    rows, width = scaled_q.shape
    blocks = rows // PIECE
    part = pl.BlockSpec((PIECE, width), lambda i: (i, 0))
    wide = pl.BlockSpec((PIECE, 3 * width), lambda i: (i, 0))
    row = pl.BlockSpec((2, blocks, PIECE), lambda i: (0, 0, 0))
    return pl.pallas_call(
        finish_kernel,
        grid=(blocks,),
        in_specs=[part, part, part, wide, row, row],
        out_specs=wide,
        out_shape=jax.ShapeDtypeStruct((rows, 3 * width), BF),
        name="finish",
    )(scaled_q, scaled_k, grad_values, raw, squares, inner)


def norm_factor(values):
    return lax.rsqrt(jnp.mean(values * values, axis=-1, keepdims=True) + epsilon)


def norm_back(values, factor, gain, cotangent):
    scaled = gain * cotangent
    inner = jnp.mean(values * scaled, axis=-1, keepdims=True)
    grad = factor * scaled - values * (factor * factor * factor) * inner
    return grad, jnp.sum(cotangent * values * factor, axis=0)


def per_device(
    hidden_in,
    piece_index,
    pad_flags,
    cotangent,
    query_weight,
    key_weight,
    value_weight,
    output_weight,
    gate_weight,
    up_weight,
    down_weight,
    query_gain,
    key_gain,
    attention_gain,
    feed_gain,
):
    shards = lax.axis_size("shard")
    planes = lax.axis_size("z")
    shard = lax.axis_index("shard")
    core = lax.axis_index("core")
    plane = lax.axis_index("z")
    tokens = hidden_in[0]
    rows, width = tokens.shape
    chunk = width // shards
    parts = 2 * shards
    head_cols = width // parts
    feed_cols = gate_weight.shape[1] // parts
    seq_len = rows * 2 * planes
    everything = 2 * rows * shards

    tie = lax.optimization_barrier

    def plane_relative(values):
        return jnp.stack(
            [
                lax.dynamic_index_in_dim(values, (shard ^ k) * 2 + (core ^ r), 0, keepdims=False)
                for r in range(2)
                for k in range(shards)
            ]
        )

    def plane_absolute(values):
        return jnp.stack(
            [
                lax.dynamic_index_in_dim(values, (core ^ r) * shards + (shard ^ j), 0, keepdims=False)
                for j in range(shards)
                for r in range(2)
            ]
        )

    def absolute_shards(blocks):
        stacked = jnp.stack(blocks)
        return jnp.stack(
            [lax.dynamic_index_in_dim(stacked, shard ^ j, 0, keepdims=False) for j in range(shards)]
        )

    info_rows = 2 * rows // chunk
    info = jnp.stack([piece_index[0], pad_flags[0]]).astype(BF).reshape(info_rows, chunk)
    info = jnp.pad(info, ((0, 16 - info_rows), (0, 0)))

    def chunk_of(k):
        return jnp.concatenate([lax.dynamic_slice_in_dim(tokens, (shard ^ k) * chunk, chunk, 1), info], 0)

    by_seq = jnp.stack([send_shard(chunk_of(k), k) if k else chunk_of(k) for k in range(shards)])
    by_plane = [
        lax.dynamic_index_in_dim(by_seq, shard ^ plane ^ k, 0, keepdims=False) for k in range(planes)
    ]
    by_plane = jnp.stack([send_plane(by_plane[k], k) if k else by_plane[k] for k in range(planes)])
    mine = by_plane[:, :rows].reshape(planes * rows, chunk)
    info_mine = by_plane[:, rows : rows + info_rows].reshape(planes, 2, rows)
    info_mine = jnp.stack(
        [lax.dynamic_index_in_dim(info_mine, plane ^ j, 0, keepdims=False) for j in range(planes)]
    )
    info_both = jnp.stack([info_mine, send_core(info_mine)], 1)
    info_seq = jnp.where(core == 0, info_both, info_both[:, ::-1]).astype(F32)
    piece_seq = info_seq[:, :, 0].reshape(seq_len)
    pad_seq = info_seq[:, :, 1].reshape(seq_len)
    block_flags = (piece_seq.reshape(-1, PIECE)[:, 0] >= 0.0).astype(jnp.int32)
    block_flags = jnp.concatenate([block_flags, core[None], plane[None]])
    key_bias = jnp.where(pad_seq > 0.0, masked_score, 0.0)[:, None]

    def column_block(weight, k, cols):
        return lax.dynamic_slice_in_dim(weight, ((shard ^ k) * 2 + core) * cols, cols, 1)

    gain_rows = jnp.pad(
        jnp.stack([attention_gain, feed_gain]), ((0, 14), (0, 3 * head_cols - attention_gain.shape[0]))
    )

    def input_block(k):
        block = [column_block(w, k, head_cols) for w in (query_weight, key_weight, value_weight)]
        return jnp.concatenate([jnp.concatenate(block, 1), gain_rows], 0)

    input_blocks = [input_block(0)] + [send_shard(input_block(k), k) for k in range(1, shards)]
    gains = absolute_shards([b[chunk : chunk + 2, : attention_gain.shape[0]] for b in input_blocks])
    gains = gains.transpose(1, 0, 2).reshape(2, width).astype(F32)
    out_block = lax.dynamic_slice_in_dim(output_weight, core * head_cols, head_cols, 0)
    down_block = lax.dynamic_slice_in_dim(down_weight, core * feed_cols, feed_cols, 0)
    query_gain_here = lax.dynamic_slice_in_dim(query_gain, core * head_cols, head_cols, 0).astype(F32)[None]
    key_gain_here = lax.dynamic_slice_in_dim(key_gain, core * head_cols, head_cols, 0).astype(F32)[None]
    rates = theta_base ** (-jnp.arange(HEAD // 2).astype(F32) * (2.0 / HEAD))
    angles = jnp.arange(seq_len, dtype=jnp.int32).astype(F32)[:, None] * rates[None, :]
    cosine, sine = jnp.cos(angles), jnp.sin(angles)
    cosine = jnp.concatenate([cosine, cosine], 1)
    sine = jnp.concatenate([-sine, sine], 1)

    gathered = gather_shard(mine)
    gate_weight, up_weight, gathered = tie((gate_weight, up_weight, gathered))
    gathered = [gathered, [send_core(block) for block in gathered]]

    def feed_block(k):
        return jnp.concatenate([column_block(w, k, feed_cols) for w in (gate_weight, up_weight)], 1)

    feed_blocks = [feed_block(0)] + [send_shard(feed_block(k), k) for k in range(1, shards - 1)]
    inputs_here = gathered
    raw, squares = project(inputs_here, input_blocks)
    squares = sum_plane(squares.reshape(2, 2, seq_len // 2), True)
    squares, feed_blocks, gate_weight, up_weight = tie((squares, feed_blocks, gate_weight, up_weight))
    feed_blocks.append(send_shard(feed_block(shards - 1), shards - 1))
    squares = squares.reshape(2, seq_len // PIECE, PIECE)
    per_block = rows // PIECE
    attended_seq, query_low, key_low, value_low, lse = attend_forward(
        raw, squares, query_gain_here, key_gain_here, cosine, sine, key_bias, block_flags, per_block
    )

    attended = lax.all_to_all(
        attended_seq.reshape(planes, 2 * rows, head_cols), "z", 0, 0, tiled=True
    ).reshape(parts, rows, head_cols)
    attended, feed_blocks = tie((attended, feed_blocks))
    attended = plane_relative(attended).reshape(everything, head_cols)
    half = everything // 2
    whole_feed = jnp.zeros((width, 2 * feed_cols), BF)
    for k in range(shards):
        whole_feed = lax.dynamic_update_slice_in_dim(whole_feed, feed_blocks[k], (shard ^ k) * chunk, 0)

    def blocks_of(values):
        return values.reshape(shards, rows, values.shape[-1])

    branch_attn = reduce_plane(
        blocks_of(mm(attended[half:], out_block)), blocks_of(mm(attended[:half], out_block))
    )
    attn_factor = norm_factor(branch_attn)
    residual = tokens.astype(F32) + branch_attn * attn_factor * gains[0]
    gathered = gather_plane(residual.astype(BF))
    residual_all = jnp.concatenate(gathered[0] + gathered[1], 0)
    gate = mm(residual_all, whole_feed[:, :feed_cols])
    up = mm(residual_all, whole_feed[:, feed_cols:])
    activated = (jax.nn.silu(gate) * up).astype(BF)
    branch_feed = reduce_plane(
        blocks_of(mm(activated[half:], down_block)), blocks_of(mm(activated[:half], down_block))
    )
    feed_factor = norm_factor(branch_feed)
    result = residual + branch_feed * feed_factor * gains[1]

    grad_out = cotangent[0].astype(F32)
    grad_feed, grad_feed_gain = norm_back(branch_feed, feed_factor, gains[1], grad_out)
    gathered = gather_plane(grad_feed.astype(BF))
    grad_feed_all = jnp.concatenate(gathered[0] + gathered[1], 0)
    grad_down = contract_rows(activated, grad_feed_all).astype(BF)
    grad_down, grad_feed_all = tie((grad_down, grad_feed_all))

    def plane_share(terms):
        flat = terms.reshape(-1, terms.shape[-1])
        share = lax.psum_scatter(flat, "z", scatter_dimension=0, tiled=True)
        return share.reshape((1,) + terms.shape[1:])[0]

    def to_owner(share, relative):
        blocks = []
        for k in range(shards):
            block = share[k] if relative else lax.dynamic_index_in_dim(share, shard ^ k, 0, keepdims=False)
            blocks.append(send_shard(block, k) if k else block)
        return absolute_shards(blocks)

    def copies(values):
        whole = lax.all_gather(values, ("z", "core"), axis=0)
        return whole.reshape((planes, 2) + values.shape)

    down_share = plane_share(grad_down.reshape(planes, feed_cols // planes, width))
    grad_act = contract_cols(grad_feed_all, down_block)
    sigmoid = jax.nn.sigmoid(gate)
    grad_gate = (grad_act * up * sigmoid * (1.0 + gate * (1.0 - sigmoid))).astype(BF)
    grad_up = (grad_act * gate * sigmoid).astype(BF)

    def feed_back(part):
        return contract_cols(grad_gate[part], whole_feed[:, :feed_cols]) + contract_cols(
            grad_up[part], whole_feed[:, feed_cols:]
        )

    got_core = send_core(feed_back(slice(half, None)).astype(BF))
    gate_terms = weight_terms(residual_all, grad_gate, shards, planes)
    gate_terms, grad_gate, grad_up, got_core = tie((gate_terms, grad_gate, grad_up, got_core))
    gate_share = plane_share(gate_terms)
    to_mine = feed_back(slice(None, half)).astype(BF)
    to_mine, got_core, grad_up = tie((to_mine, got_core, grad_up))
    up_terms = weight_terms(residual_all, grad_up, shards, planes)
    up_share = plane_share(up_terms)

    def feed_term(k, part):
        return blocks_of(to_mine)[k, part].astype(F32) + blocks_of(got_core)[k, part].astype(F32)

    feed_term.rows = rows
    grad_feed_in = reduce_shard(feed_term)
    grad_feed_in, down_share, up_terms = tie((grad_feed_in, down_share, up_terms))

    grad_resid = grad_out + grad_feed_in
    grad_branch, grad_attention_gain = norm_back(branch_attn, attn_factor, gains[0], grad_resid)
    gathered = gather_plane(grad_branch.astype(BF))
    grad_branch_all = jnp.concatenate(gathered[0] + gathered[1], 0)
    grad_mixed = contract_cols(grad_branch_all, out_block).astype(BF)
    grad_mixed = plane_absolute(grad_mixed.reshape(parts, rows, head_cols))
    grad_mixed = lax.all_to_all(
        grad_mixed.reshape(shards, 2 * rows, head_cols), "z", 0, 0, tiled=True
    ).reshape(seq_len, head_cols)
    grad_output = contract_rows(attended, grad_branch_all).astype(BF)
    grad_output, grad_mixed, gate_share = tie((grad_output, grad_mixed, gate_share))
    output_share = plane_share(grad_output.reshape(planes, head_cols // planes, width))
    scaled_q, scaled_k, grad_values, inner, grad_gains = attend_backward(
        query_low, key_low, value_low, grad_mixed, attended_seq, raw, squares, query_gain_here, key_gain_here,
        cosine, sine, key_bias, block_flags, lse, per_block,
    )
    inner, up_share = tie((inner, up_share))
    inner = sum_plane(jnp.sum(inner, 0).reshape(2, 2, seq_len // 2), True).reshape(squares.shape)
    grad_raw = finish(scaled_q, scaled_k, grad_values, raw, squares, inner)
    input_part = input_terms(inputs_here, grad_raw, planes)
    grad_raw, input_part = tie((grad_raw, input_part))
    input_share = plane_share(input_part)
    seq_half = seq_len // 2

    def chunks_of(values):
        return jnp.stack([contract_cols(values, block[:chunk]) for block in input_blocks])

    grad_chunk = reduce_plane(chunks_of(grad_raw[seq_half:]), chunks_of(grad_raw[:seq_half]))
    grad_chunk = grad_chunk.astype(BF).reshape(planes, rows, chunk)
    grad_chunk = jnp.stack([send_plane(grad_chunk[k], k) if k else grad_chunk[k] for k in range(planes)])
    by_shard = [
        lax.dynamic_index_in_dim(grad_chunk, shard ^ plane ^ k, 0, keepdims=False) for k in range(shards)
    ]
    by_shard = [send_shard(by_shard[k], k) if k else by_shard[k] for k in range(shards)]
    grad_chunk = absolute_shards(by_shard)
    grad_tokens = grad_resid + grad_chunk.transpose(1, 0, 2).reshape(rows, width).astype(F32)

    grad_down_weight = rows_out(copies(down_share))
    (grad_gate_weight,) = columns_out(copies(to_owner(gate_share, False)), 1)
    (grad_up_weight,) = columns_out(copies(to_owner(up_share, False)), 1)
    grad_output_weight = rows_out(copies(output_share))
    grad_query_weight, grad_key_weight, grad_value_weight = columns_out(copies(to_owner(input_share, True)), 3)

    valid = (pad_flags[0] == 0).astype(F32)[:, None]
    stat_terms = jnp.stack(
        [
            jnp.sum(valid * result * result),
            jnp.sum(valid * branch_attn * branch_attn),
            jnp.sum(valid * branch_feed * branch_feed),
            jnp.sum(valid),
        ]
    )
    terms = jnp.concatenate([grad_attention_gain, grad_feed_gain, jnp.pad(stat_terms, (0, 124))])
    terms = sum_over_planes(sum_plane(terms.reshape(-1, 128))).reshape(-1)
    gain_width = query_gain.shape[0]
    gain_full = terms[: 2 * width].reshape(2, width)
    gain_full = lax.dynamic_slice_in_dim(gain_full, shard * gain_width, gain_width, 1)
    stat_terms = terms[2 * width :]
    stats = jnp.sqrt(stat_terms[:3] / (stat_terms[3] * width))
    gain_heads = sum_over_planes(grad_gains.transpose(1, 0, 2).reshape(2, head_cols))
    gain_other = send_core(gain_heads)
    gain_heads = jnp.where(
        core == 0,
        jnp.concatenate([gain_heads, gain_other], 1),
        jnp.concatenate([gain_other, gain_heads], 1),
    )
    return (
        result[None],
        grad_tokens[None],
        grad_query_weight,
        grad_key_weight,
        grad_value_weight,
        grad_output_weight,
        grad_gate_weight,
        grad_up_weight,
        grad_down_weight,
        gain_heads[0],
        gain_heads[1],
        gain_full[0],
        gain_full[1],
        stats,
    )


def solution(mesh):
    devices = mesh.devices.reshape(mesh.shape["replica"] // 2, 2, mesh.shape["shard"])
    split = Mesh(devices, ("z", "core", "shard"))
    tokens = ("z", "core")
    placed = (
        (P("shard", tokens, None), P("shard", tokens), P("shard", tokens), P("shard", tokens, None))
        + (P("shard", None),) * 7
        + (P("shard"),) * 4
    )
    return jax.shard_map(
        per_device,
        mesh=split,
        in_specs=placed,
        out_specs=(P("shard", tokens, None),) * 2
        + (P("shard", None),) * 7
        + (P("shard"),) * 4
        + (P(),),
        check_vma=False,
    )
```

```python
import functools

import jax
import jax.numpy as jnp
from jax import lax
from jax.experimental import pallas as pl
from jax.experimental.pallas import tpu as pltpu
from jax.sharding import Mesh, PartitionSpec as P

HEADS = 16
HEAD = 128
PIECE = 256

epsilon = 1e-06
theta_base = 500000.0
masked_score = -1e30
score_scale = HEAD ** (-0.5)

BF = jnp.bfloat16
F32 = jnp.float32


def mm(left, right):
    return jnp.dot(left, right, preferred_element_type=F32)


def contract_rows(left, right):
    return lax.dot_general(left, right, (((0,), (0,)), ((), ())), preferred_element_type=F32)


def contract_cols(left, right):
    return lax.dot_general(left, right, (((1,), (1,)), ((), ())), preferred_element_type=F32)


def send_core(values):
    return lax.ppermute(values, "core", [(0, 1), (1, 0)])


def send_shard(values, k):
    count = lax.axis_size("shard")
    return lax.ppermute(values, "shard", [(i, i ^ k) for i in range(count)])


def send_plane(values, k):
    count = lax.axis_size("z")
    return lax.ppermute(values, "z", [(i, i ^ k) for i in range(count)])


def gather_shard(values):
    count = lax.axis_size("shard")
    if count != 4:
        return [values] + [send_shard(values, k) for k in range(1, count)]
    half = values.shape[0] // 2
    from_x = send_shard(values, 1)
    from_y = send_shard(values, 2)
    far_a = send_shard(from_x[:half], 2)
    far_b = send_shard(from_y[half:], 1)
    return [values, from_x, from_y, jnp.concatenate([far_a, far_b], 0)]


def gather_plane(values):
    mine = gather_shard(values)
    return [mine, [send_core(block) for block in mine]]


def reduce_steps(term):
    count = lax.axis_size("shard")
    everything = slice(None)
    if count != 4:
        got = yield [send_shard(term(k, everything).astype(BF), k) for k in range(1, count)]
        result = term(0, everything)
        for values in got:
            result = result + values.astype(F32)
        return result
    near, far = slice(0, term.rows // 2), slice(term.rows // 2, None)
    via_x, via_y = yield (send_shard(term(3, near).astype(BF), 1), send_shard(term(3, far).astype(BF), 2))
    to_y = jnp.concatenate([(term(2, near) + via_x.astype(F32)).astype(BF), term(2, far).astype(BF)], 0)
    to_x = jnp.concatenate([term(1, near).astype(BF), (term(1, far) + via_y.astype(F32)).astype(BF)], 0)
    from_x, from_y = yield (send_shard(to_x, 1), send_shard(to_y, 2))
    return term(0, everything) + from_x.astype(F32) + from_y.astype(F32)


def run_steps(steps, between=lambda values: values):
    values = next(steps)
    while True:
        try:
            values = steps.send(between(values))
        except StopIteration as stop:
            return stop.value


def reduce_shard(term):
    return run_steps(reduce_steps(term))


def reduce_plane(other, mine, also):
    got = send_core(other.astype(BF))
    mine, got, also = lax.optimization_barrier((mine.astype(BF), got, also))

    def term(k, part):
        return mine[k, part].astype(F32) + got[k, part].astype(F32)

    term.rows = mine.shape[1]
    return reduce_shard(term), also


def sum_over_planes(values):
    parts = [send_plane(values, k) for k in range(1, lax.axis_size("z"))]
    return sum(parts, values)


def sum_plane(values, swapped=False):
    count = lax.axis_size("shard")
    other = send_core(values)
    values = values + (other[:, ::-1] if swapped else other)
    step = 1
    while step < count:
        values = values + send_shard(values, step)
        step *= 2
    return values


def terms_kernel(tokens, grads, out):
    total = contract_rows(tokens[...], grads[...]).astype(BF)
    out[...] = total.reshape(out.shape)


def weight_terms(tokens, grads, shards, planes):
    rows, width = tokens.shape
    cols = grads.shape[1]
    chunk = width // shards
    return pl.pallas_call(
        terms_kernel,
        grid=(shards,),
        in_specs=[
            pl.BlockSpec((rows, chunk), lambda i: (0, i)),
            pl.BlockSpec((rows, cols), lambda i: (0, 0), pipeline_mode=pl.Buffered(1)),
        ],
        out_specs=pl.BlockSpec((planes, 1, chunk // planes, cols), lambda i: (0, i, 0, 0)),
        out_shape=jax.ShapeDtypeStruct((planes, shards, chunk // planes, cols), BF),
        compiler_params=pltpu.CompilerParams(vmem_limit_bytes=40 * 1024 * 1024),
        name="weight_terms",
    )(tokens, grads)


def columns_kernel(copies, *outs):
    _, cores, shards, rows, cols = copies.shape
    share = cols // len(outs)
    for n, out in enumerate(outs):
        for s in range(shards):
            for c in range(cores):
                at = (s * cores + c) * share
                out[:, at : at + share] = copies[0, c, s, :, n * share : (n + 1) * share].astype(F32)


def columns_out(copies, count):
    planes, cores, shards, rows, cols = copies.shape
    wide = shards * cores * cols // count
    return pl.pallas_call(
        columns_kernel,
        grid=(planes,),
        in_specs=[pl.BlockSpec((1,) + copies.shape[1:], lambda i: (i, 0, 0, 0, 0))],
        out_specs=[pl.BlockSpec((rows, wide), lambda i: (i, 0))] * count,
        out_shape=[jax.ShapeDtypeStruct((planes * rows, wide), F32)] * count,
        compiler_params=pltpu.CompilerParams(vmem_limit_bytes=40 * 1024 * 1024),
        name="columns_out",
    )(copies)


def rows_kernel(copies, out):
    out[...] = copies[0, 0].astype(F32)


def rows_out(copies):
    planes, cores, rows, cols = copies.shape
    return pl.pallas_call(
        rows_kernel,
        grid=(planes, cores),
        in_specs=[pl.BlockSpec((1, 1, rows, cols), lambda i, j: (i, j, 0, 0))],
        out_specs=pl.BlockSpec((rows, cols), lambda i, j: (j * planes + i, 0)),
        out_shape=jax.ShapeDtypeStruct((planes * cores * rows, cols), F32),
        name="rows_out",
    )(copies)


def project_kernel(count, *refs):
    tokens, weights, raw, squares = refs[: 2 * count], refs[2 * count : 3 * count], refs[-2], refs[-1]
    chunk = tokens[0].shape[1]
    third = raw.shape[1] // 3
    block = pl.program_id(0) * pl.num_programs(1) + pl.program_id(1)
    for r in range(2):

        @pl.when(pl.program_id(0) == r)
        def _():
            total = mm(tokens[r * count][...], weights[0][:chunk, :])
            for k in range(1, count):
                total += mm(tokens[r * count + k][...], weights[k][:chunk, :])
            raw[...] = total
            for n in range(2):
                squared = total[:, n * third : (n + 1) * third]
                squared = squared * squared
                folded = squared[:, :HEAD]
                for h in range(1, third // HEAD):
                    folded += squared[:, h * HEAD : (h + 1) * HEAD]
                squares[n, pl.ds(block, 1), :] = as_row(folded)


def project(pieces, weights):
    count = len(weights)
    rows, chunk = pieces[0][0].shape
    cols = weights[0].shape[1]
    steps = rows // PIECE

    def spec(r):
        return pl.BlockSpec((PIECE, chunk), lambda a, i: (jnp.where(a == r, i, (steps - 1) * (a > r)), 0))

    return pl.pallas_call(
        functools.partial(project_kernel, count),
        grid=(2, steps),
        in_specs=[spec(r) for r in range(2) for _ in range(count)]
        + [pl.BlockSpec(w.shape, lambda a, i: (0, 0), pipeline_mode=pl.Buffered(1)) for w in weights],
        out_specs=[
            pl.BlockSpec((PIECE, cols), lambda a, i: (a * steps + i, 0)),
            pl.BlockSpec((2, 2 * steps, PIECE), lambda a, i: (0, 0, 0)),
        ],
        out_shape=[
            jax.ShapeDtypeStruct((2 * rows, cols), F32),
            jax.ShapeDtypeStruct((2, 2 * steps, PIECE), F32),
        ],
        compiler_params=pltpu.CompilerParams(vmem_limit_bytes=40 * 1024 * 1024),
        name="project",
    )(*pieces[0], *pieces[1], *weights)


def input_terms_kernel(count, *refs):
    tokens, grads, out = refs[: 2 * count], refs[2 * count], refs[2 * count + 1]
    rows = tokens[0].shape[0]
    planes, _, _, share, third = out.shape
    for k in range(count):
        total = contract_rows(tokens[k][...], grads[:rows, :]) + contract_rows(tokens[count + k][...], grads[rows:, :])
        for n in range(3):
            out[:, k, n] = total[:, n * third : (n + 1) * third].astype(BF).reshape(planes, share, third)


def input_terms(pieces, grads, planes):
    count = len(pieces[0])
    chunk = pieces[0][0].shape[1]
    return pl.pallas_call(
        functools.partial(input_terms_kernel, count),
        out_shape=jax.ShapeDtypeStruct((planes, count, 3, chunk // planes, grads.shape[1] // 3), BF),
        compiler_params=pltpu.CompilerParams(vmem_limit_bytes=56 * 1024 * 1024),
        name="input_terms",
    )(*pieces[0], *pieces[1], grads)


def attention_out_kernel(shards, share, copies, query, key, value, output):
    _, cores, _, cols = copies.shape
    for n, out in enumerate((query, key, value)):
        for s in range(shards):
            for c in range(cores):
                at = (s * cores + c) * cols
                row = (s * 3 + n) * share
                out[:, at : at + cols] = copies[0, c, row : row + share, :].astype(F32)
    first = shards * 3 * share
    rows = output.shape[1]
    for c in range(cores):
        for j in range(output.shape[2] // cols):
            row = first + j * rows
            output[c, :, j * cols : (j + 1) * cols] = copies[0, c, row : row + rows, :].astype(F32)


def attention_out(copies, shards, share):
    planes, cores, total, cols = copies.shape
    wide = shards * cores * cols
    rows = (total - shards * 3 * share) * cols // wide
    return pl.pallas_call(
        functools.partial(attention_out_kernel, shards, share),
        grid=(planes,),
        in_specs=[pl.BlockSpec((1, cores, total, cols), lambda i: (i, 0, 0, 0))],
        out_specs=[pl.BlockSpec((share, wide), lambda i: (i, 0))] * 3
        + [pl.BlockSpec((cores, rows, wide), lambda i: (0, i, 0))],
        out_shape=[jax.ShapeDtypeStruct((planes * share, wide), F32)] * 3
        + [jax.ShapeDtypeStruct((cores, planes * rows, wide), F32)],
        compiler_params=pltpu.CompilerParams(vmem_limit_bytes=40 * 1024 * 1024),
        name="attention_out",
    )(copies)


def memory_block(block, where, blocks, per_device):
    core, here = where
    plane, rest = divmod(block, 2 * per_device)
    which, inside = divmod(rest, per_device)
    return (which ^ core) * (blocks // 2) + (plane ^ here) * per_device + inside


def as_columns(row):
    return jnp.broadcast_to(row, (HEAD, PIECE)).T


def as_row(values):
    return jnp.sum(values.T, axis=0, keepdims=True)


def factor_of(squares):
    return lax.rsqrt(squares * (1.0 / (HEADS * HEAD)) + epsilon)


def forward_kernel(
    per_device, flags, raw_q, raw_k, raw_v, squares, gain_q, gain_k, cosine, sine, key_bias,
    mixed, queries, keys, values, lse,
):
    rows = queries.shape[0]
    blocks = rows // PIECE
    core = (flags[blocks], flags[blocks + 1])
    place_key = lax.broadcasted_iota(jnp.int32, (PIECE, PIECE), 0)
    place_query = lax.broadcasted_iota(jnp.int32, (PIECE, PIECE), 1)
    causal = place_key <= place_query
    for b in range(blocks):
        here = pl.ds(b * PIECE, PIECE)
        from_block = memory_block(b, core, blocks, per_device)
        there = pl.ds(pl.multiple_of(from_block * PIECE, PIECE), PIECE)
        for n, (raw, gain, turned) in enumerate(((raw_q, gain_q, queries), (raw_k, gain_k, keys))):
            factor = as_columns(factor_of(squares[n, pl.ds(from_block, 1), :]))
            normed = raw[there, :] * factor * gain[...]
            turned[here, :] = (
                normed * cosine[here, :] + pltpu.roll(normed, HEAD // 2, 1) * sine[here, :]
            ).astype(BF)
        values[here, :] = raw_v[there, :].astype(BF)
    for b in range(blocks):
        here = pl.ds(b * PIECE, PIECE)
        seen = pl.ds(0, (b + 1) * PIECE)
        whole = flags[b] > 0
        scores = contract_cols(keys[seen, :], queries[here, :]) * score_scale + key_bias[seen, :]
        last = jnp.where(causal | whole, scores[b * PIECE :], masked_score)
        scores = jnp.concatenate([scores[: b * PIECE], last], 0) if b else last
        highest = jnp.max(scores, axis=0, keepdims=True)
        raised = jnp.exp(scores - highest)
        summed = jnp.sum(raised, axis=0, keepdims=True)
        lse[:, here] = highest + jnp.log(summed)
        probs = (raised * (1.0 / summed)).astype(BF)
        mixed[here, :] = contract_rows(probs, values[seen, :]).astype(mixed.dtype)


def attend_forward(raw, squares, gain_q, gain_k, cosine, sine, key_bias, flags, per_device):
    rows = raw.shape[0]
    heads = raw.shape[1] // (3 * HEAD)
    blocks = rows // PIECE
    column = pl.BlockSpec((rows, HEAD), lambda h, f: (0, h))
    table = pl.BlockSpec((rows, HEAD), lambda h, f: (0, 0), pipeline_mode=pl.Buffered(1))
    gain = pl.BlockSpec((1, HEAD), lambda h, f: (0, h))
    turned = jax.ShapeDtypeStruct((rows, heads * HEAD), BF)
    return pl.pallas_call(
        functools.partial(forward_kernel, per_device),
        grid_spec=pltpu.PrefetchScalarGridSpec(
            num_scalar_prefetch=1,
            grid=(heads,),
            in_specs=[
                column,
                pl.BlockSpec((rows, HEAD), lambda h, f: (0, heads + h)),
                pl.BlockSpec((rows, HEAD), lambda h, f: (0, 2 * heads + h)),
                pl.BlockSpec((2, blocks, PIECE), lambda h, f: (0, 0, 0)),
                gain,
                gain,
                table,
                table,
                pl.BlockSpec((rows, 1), lambda h, f: (0, 0), pipeline_mode=pl.Buffered(1)),
            ],
            out_specs=[column] * 4 + [pl.BlockSpec((None, 1, rows), lambda h, f: (h, 0, 0))],
        ),
        out_shape=[turned] * 4 + [jax.ShapeDtypeStruct((heads, 1, rows), F32)],
        compiler_params=pltpu.CompilerParams(vmem_limit_bytes=52 * 1024 * 1024),
        name="attend_forward",
    )(flags, raw, raw, raw, squares, gain_q, gain_k, cosine, sine, key_bias)


def backward_kernel(
    per_device, flags, queries, keys, values, grad_mixed, mixed, raw_q, raw_k, squares, gain_q, gain_k,
    cosine, sine, key_bias, lse,
    scaled_q, scaled_k, grad_values, inner, grad_gains, keys_acc, values_acc,
):
    rows = queries.shape[0]
    blocks = rows // PIECE
    core = (flags[blocks], flags[blocks + 1])
    place_key = lax.broadcasted_iota(jnp.int32, (PIECE, PIECE), 0)
    place_query = lax.broadcasted_iota(jnp.int32, (PIECE, PIECE), 1)
    causal = place_key <= place_query
    keys_acc[...] = jnp.zeros_like(keys_acc)
    values_acc[...] = jnp.zeros_like(values_acc)
    grad_gains[...] = jnp.zeros_like(grad_gains)

    def turn_back(n, b, grad, raw, gain, scaled_out):
        here = pl.ds(b * PIECE, PIECE)
        block = memory_block(b, core, blocks, per_device)
        there = pl.ds(pl.multiple_of(block * PIECE, PIECE), PIECE)
        turned = grad * cosine[here, :] - pltpu.roll(grad, HEAD // 2, 1) * sine[here, :]
        raw_block = raw[there, :]
        scaled = turned * gain[...]
        scaled_out[there, :] = scaled
        inner[n, pl.ds(block, 1), :] = as_row(raw_block * scaled)
        factor = as_columns(factor_of(squares[n, pl.ds(block, 1), :]))
        grad_gains[n : n + 1, :] += jnp.sum(turned * raw_block * factor, axis=0, keepdims=True)

    for b in range(blocks):
        here = pl.ds(b * PIECE, PIECE)
        whole = flags[b] > 0
        query_block = queries[here, :]
        grad_block = grad_mixed[here, :]
        delta = as_row(grad_block.astype(F32) * mixed[here, :].astype(F32))
        grad_query = jnp.zeros((PIECE, HEAD), F32)
        for first in range(0, b + 1, 8):
            last = min(first + 8, b + 1)
            seen = pl.ds(first * PIECE, (last - first) * PIECE)
            scores = contract_cols(keys[seen, :], query_block) * score_scale + key_bias[seen, :]
            if last == b + 1:
                edge = (b - first) * PIECE
                final = jnp.where(causal | whole, scores[edge:], masked_score)
                scores = jnp.concatenate([scores[:edge], final], 0) if edge else final
            probs = jnp.exp(scores - lse[:, here])
            grad_probs = contract_cols(values[seen, :], grad_block)
            grad_scores = (probs * (grad_probs - delta)).astype(BF)
            values_acc[seen, :] += mm(probs.astype(BF), grad_block)
            keys_acc[seen, :] += mm(grad_scores, query_block)
            grad_query += contract_rows(grad_scores, keys[seen, :])
        turn_back(0, b, grad_query * score_scale, raw_q, gain_q, scaled_q)
    for b in range(blocks):
        here = pl.ds(b * PIECE, PIECE)
        turn_back(1, b, keys_acc[here, :] * score_scale, raw_k, gain_k, scaled_k)
        block = memory_block(b, core, blocks, per_device)
        there = pl.ds(pl.multiple_of(block * PIECE, PIECE), PIECE)
        grad_values[there, :] = values_acc[here, :].astype(BF)


def attend_backward(
    queries, keys, values, grad_mixed, mixed, raw, squares, gain_q, gain_k, cosine, sine, key_bias, flags, lse,
    per_device,
):
    rows, width = queries.shape
    heads = width // HEAD
    blocks = rows // PIECE
    column = pl.BlockSpec((rows, HEAD), lambda h, f: (0, h))
    table = pl.BlockSpec((rows, HEAD), lambda h, f: (0, 0), pipeline_mode=pl.Buffered(1))
    gain = pl.BlockSpec((1, HEAD), lambda h, f: (0, h))
    return pl.pallas_call(
        functools.partial(backward_kernel, per_device),
        grid_spec=pltpu.PrefetchScalarGridSpec(
            num_scalar_prefetch=1,
            grid=(heads,),
            in_specs=[column] * 5
            + [
                column,
                pl.BlockSpec((rows, HEAD), lambda h, f: (0, heads + h)),
                pl.BlockSpec((2, blocks, PIECE), lambda h, f: (0, 0, 0)),
                gain,
                gain,
                table,
                table,
                pl.BlockSpec((rows, 1), lambda h, f: (0, 0), pipeline_mode=pl.Buffered(1)),
                pl.BlockSpec((None, 1, rows), lambda h, f: (h, 0, 0)),
            ],
            out_specs=[column] * 3
            + [
                pl.BlockSpec((None, 2, blocks, PIECE), lambda h, f: (h, 0, 0, 0)),
                pl.BlockSpec((None, 2, HEAD), lambda h, f: (h, 0, 0)),
            ],
            scratch_shapes=[pltpu.VMEM((rows, HEAD), F32)] * 2,
        ),
        out_shape=[
            jax.ShapeDtypeStruct((rows, width), F32),
            jax.ShapeDtypeStruct((rows, width), F32),
            jax.ShapeDtypeStruct((rows, width), BF),
            jax.ShapeDtypeStruct((heads, 2, blocks, PIECE), F32),
            jax.ShapeDtypeStruct((heads, 2, HEAD), F32),
        ],
        compiler_params=pltpu.CompilerParams(vmem_limit_bytes=56 * 1024 * 1024),
        name="attend_backward",
    )(
        flags, queries, keys, values, grad_mixed, mixed, raw, raw, squares, gain_q, gain_k, cosine, sine,
        key_bias, lse,
    )


def finish_kernel(scaled_q, scaled_k, grad_values, raw, squares, inner, out):
    block = pl.program_id(0)
    width = scaled_q.shape[1]
    for n, scaled in enumerate((scaled_q, scaled_k)):
        factor_row = factor_of(squares[n, pl.ds(block, 1), :])
        inner_row = inner[n, pl.ds(block, 1), :] * (1.0 / (HEADS * HEAD))
        factor = as_columns(factor_row)
        slope = as_columns(factor_row * factor_row * factor_row * inner_row)
        for h in range(width // HEAD):
            at = n * width + h * HEAD
            out[:, at : at + HEAD] = (
                factor * scaled[:, h * HEAD : (h + 1) * HEAD] - raw[:, at : at + HEAD] * slope
            ).astype(BF)
    out[:, 2 * width :] = grad_values[...]


def finish(scaled_q, scaled_k, grad_values, raw, squares, inner):
    rows, width = scaled_q.shape
    blocks = rows // PIECE
    part = pl.BlockSpec((PIECE, width), lambda i: (i, 0))
    wide = pl.BlockSpec((PIECE, 3 * width), lambda i: (i, 0))
    row = pl.BlockSpec((2, blocks, PIECE), lambda i: (0, 0, 0))
    return pl.pallas_call(
        finish_kernel,
        grid=(blocks,),
        in_specs=[part, part, part, wide, row, row],
        out_specs=wide,
        out_shape=jax.ShapeDtypeStruct((rows, 3 * width), BF),
        name="finish",
    )(scaled_q, scaled_k, grad_values, raw, squares, inner)


def norm_factor(values):
    return lax.rsqrt(jnp.mean(values * values, axis=-1, keepdims=True) + epsilon)


def norm_back(values, factor, gain, cotangent):
    scaled = gain * cotangent
    inner = jnp.mean(values * scaled, axis=-1, keepdims=True)
    grad = factor * scaled - values * (factor * factor * factor) * inner
    return grad, jnp.sum(cotangent * values * factor, axis=0)


def per_device(
    hidden_in,
    piece_index,
    pad_flags,
    cotangent,
    query_weight,
    key_weight,
    value_weight,
    output_weight,
    gate_weight,
    up_weight,
    down_weight,
    query_gain,
    key_gain,
    attention_gain,
    feed_gain,
):
    shards = lax.axis_size("shard")
    planes = lax.axis_size("z")
    shard = lax.axis_index("shard")
    core = lax.axis_index("core")
    plane = lax.axis_index("z")
    tokens = hidden_in[0]
    rows, width = tokens.shape
    chunk = width // shards
    parts = 2 * shards
    head_cols = width // parts
    feed_cols = gate_weight.shape[1] // parts
    seq_len = rows * 2 * planes
    everything = 2 * rows * shards

    tie = lax.optimization_barrier

    def plane_relative(values):
        return jnp.stack(
            [
                lax.dynamic_index_in_dim(values, (shard ^ k) * 2 + (core ^ r), 0, keepdims=False)
                for r in range(2)
                for k in range(shards)
            ]
        )

    def plane_absolute(values):
        return jnp.stack(
            [
                lax.dynamic_index_in_dim(values, (core ^ r) * shards + (shard ^ j), 0, keepdims=False)
                for j in range(shards)
                for r in range(2)
            ]
        )

    def absolute_shards(blocks):
        stacked = jnp.stack(blocks)
        return jnp.stack(
            [lax.dynamic_index_in_dim(stacked, shard ^ j, 0, keepdims=False) for j in range(shards)]
        )

    def column_block(weight, k, cols):
        return lax.dynamic_slice_in_dim(weight, ((shard ^ k) * 2 + core) * cols, cols, 1)

    gain_rows = jnp.pad(
        jnp.stack([attention_gain, feed_gain]), ((0, 14), (0, 3 * head_cols - attention_gain.shape[0]))
    )

    def input_block(k):
        block = [column_block(w, k, head_cols) for w in (query_weight, key_weight, value_weight)]
        return jnp.concatenate([jnp.concatenate(block, 1), gain_rows], 0)

    input_blocks = [input_block(0)] + [send_shard(input_block(k), k) for k in range(1, shards)]
    info_rows = 2 * rows // chunk
    info = jnp.stack([piece_index[0], pad_flags[0]]).astype(BF).reshape(info_rows, chunk)
    info = jnp.pad(info, ((0, 16 - info_rows), (0, 0)))

    def chunk_of(k):
        return jnp.concatenate([lax.dynamic_slice_in_dim(tokens, (shard ^ k) * chunk, chunk, 1), info], 0)

    by_seq = jnp.stack([send_shard(chunk_of(k), k) if k else chunk_of(k) for k in range(shards)])
    by_plane = [
        lax.dynamic_index_in_dim(by_seq, shard ^ plane ^ k, 0, keepdims=False) for k in range(planes)
    ]
    by_plane = jnp.stack([send_plane(by_plane[k], k) if k else by_plane[k] for k in range(planes)])
    rates = theta_base ** (-jnp.arange(HEAD // 2).astype(F32) * (2.0 / HEAD))
    angles = jnp.arange(seq_len, dtype=jnp.int32).astype(F32)[:, None] * rates[None, :]
    cosine, sine = jnp.cos(angles), jnp.sin(angles)
    cosine = jnp.concatenate([cosine, cosine], 1)
    sine = jnp.concatenate([-sine, sine], 1)
    by_plane, input_blocks, cosine, sine = tie((by_plane, input_blocks, cosine, sine))
    mine = by_plane[:, :rows].reshape(planes * rows, chunk)
    info_mine = by_plane[:, rows : rows + info_rows].reshape(planes, 2, rows)
    info_mine = jnp.stack(
        [lax.dynamic_index_in_dim(info_mine, plane ^ j, 0, keepdims=False) for j in range(planes)]
    )
    info_both = jnp.stack([info_mine, send_core(info_mine)], 1)
    info_seq = jnp.where(core == 0, info_both, info_both[:, ::-1]).astype(F32)
    piece_seq = info_seq[:, :, 0].reshape(seq_len)
    pad_seq = info_seq[:, :, 1].reshape(seq_len)
    block_flags = (piece_seq.reshape(-1, PIECE)[:, 0] >= 0.0).astype(jnp.int32)
    block_flags = jnp.concatenate([block_flags, core[None], plane[None]])
    key_bias = jnp.where(pad_seq > 0.0, masked_score, 0.0)[:, None]

    gains = absolute_shards([b[chunk : chunk + 2, : attention_gain.shape[0]] for b in input_blocks])
    gains = gains.transpose(1, 0, 2).reshape(2, width).astype(F32)
    out_block = lax.dynamic_slice_in_dim(output_weight, core * head_cols, head_cols, 0)
    down_block = lax.dynamic_slice_in_dim(down_weight, core * feed_cols, feed_cols, 0)
    query_gain_here = lax.dynamic_slice_in_dim(query_gain, core * head_cols, head_cols, 0).astype(F32)[None]
    key_gain_here = lax.dynamic_slice_in_dim(key_gain, core * head_cols, head_cols, 0).astype(F32)[None]

    def feed_block(k):
        return [column_block(w, k, feed_cols) for w in (gate_weight, up_weight)]

    last = shards - 1
    feed_own = [jnp.concatenate(feed_block(k), 1) for k in range(last)]
    feed_last = feed_block(last)
    gathered = gather_shard(mine)
    feed_own, feed_last, gathered = tie((feed_own, feed_last, gathered))
    gathered = [gathered, [send_core(block) for block in gathered]]
    gate_last = send_shard(feed_last[0], last)

    inputs_here = gathered
    raw, squares = project(inputs_here, input_blocks)
    squares = sum_plane(squares.reshape(2, 2, seq_len // 2), True)
    squares, gate_last, feed_own, feed_last = tie((squares, gate_last, feed_own, feed_last))
    feed_blocks = feed_own[:1] + [send_shard(feed_own[k], k) for k in range(1, last)]
    up_last = send_shard(feed_last[1], last)
    squares = squares.reshape(2, seq_len // PIECE, PIECE)
    per_block = rows // PIECE
    attended_seq, query_low, key_low, value_low, lse = attend_forward(
        raw, squares, query_gain_here, key_gain_here, cosine, sine, key_bias, block_flags, per_block
    )

    attended = lax.all_to_all(
        attended_seq.reshape(planes, 2 * rows, head_cols), "z", 0, 0, tiled=True
    ).reshape(parts, rows, head_cols)
    attended, feed_blocks = tie((attended, feed_blocks))
    attended = plane_relative(attended).reshape(everything, head_cols)
    half = everything // 2

    def blocks_of(values):
        return values.reshape(shards, rows, values.shape[-1])

    branch_attn, up_last = reduce_plane(
        blocks_of(mm(attended[half:], out_block)), blocks_of(mm(attended[:half], out_block)), up_last
    )
    feed_blocks.append(jnp.concatenate([gate_last, up_last], 1))
    whole_feed = jnp.zeros((width, 2 * feed_cols), BF)
    for k in range(shards):
        whole_feed = lax.dynamic_update_slice_in_dim(whole_feed, feed_blocks[k], (shard ^ k) * chunk, 0)
    attn_factor = norm_factor(branch_attn)
    residual = tokens.astype(F32) + branch_attn * attn_factor * gains[0]
    gathered = gather_plane(residual.astype(BF))
    residual_all = jnp.concatenate(gathered[0] + gathered[1], 0)
    gate = mm(residual_all, whole_feed[:, :feed_cols])
    up = mm(residual_all, whole_feed[:, feed_cols:])
    activated = (jax.nn.silu(gate) * up).astype(BF)
    branch_feed, _ = reduce_plane(
        blocks_of(mm(activated[half:], down_block)), blocks_of(mm(activated[:half], down_block)), ()
    )
    feed_factor = norm_factor(branch_feed)
    result = residual + branch_feed * feed_factor * gains[1]

    grad_out = cotangent[0].astype(F32)
    grad_feed, grad_feed_gain = norm_back(branch_feed, feed_factor, gains[1], grad_out)
    gathered = gather_plane(grad_feed.astype(BF))
    grad_feed_all = jnp.concatenate(gathered[0] + gathered[1], 0)
    grad_down = contract_rows(activated, grad_feed_all).astype(BF)
    grad_down, grad_feed_all = tie((grad_down, grad_feed_all))

    def plane_share(terms):
        flat = terms.reshape(-1, terms.shape[-1])
        share = lax.psum_scatter(flat, "z", scatter_dimension=0, tiled=True)
        return share.reshape((1,) + terms.shape[1:])[0]

    def to_owner(share, relative):
        blocks = []
        for k in range(shards):
            block = share[k] if relative else lax.dynamic_index_in_dim(share, shard ^ k, 0, keepdims=False)
            blocks.append(send_shard(block, k) if k else block)
        return absolute_shards(blocks)

    def copies(values):
        whole = lax.all_gather(values, ("z", "core"), axis=0)
        return whole.reshape((planes, 2) + values.shape)

    down_share = plane_share(grad_down.reshape(planes, feed_cols // planes, width))
    grad_act = contract_cols(grad_feed_all, down_block)
    sigmoid = jax.nn.sigmoid(gate)
    grad_gate = (grad_act * up * sigmoid * (1.0 + gate * (1.0 - sigmoid))).astype(BF)
    grad_up = (grad_act * gate * sigmoid).astype(BF)

    def feed_back(part):
        return contract_cols(grad_gate[part], whole_feed[:, :feed_cols]) + contract_cols(
            grad_up[part], whole_feed[:, feed_cols:]
        )

    got_core = send_core(feed_back(slice(half, None)).astype(BF))
    gate_terms = weight_terms(residual_all, grad_gate, shards, planes)
    gate_terms, grad_gate, grad_up, got_core = tie((gate_terms, grad_gate, grad_up, got_core))
    gate_share = plane_share(gate_terms)
    to_mine = feed_back(slice(None, half)).astype(BF)
    to_mine, got_core, grad_up = tie((to_mine, got_core, grad_up))
    up_terms = weight_terms(residual_all, grad_up, shards, planes)
    up_share = plane_share(up_terms)

    def feed_term(k, part):
        return blocks_of(to_mine)[k, part].astype(F32) + blocks_of(got_core)[k, part].astype(F32)

    feed_term.rows = rows
    grad_feed_in = reduce_shard(feed_term)
    grad_feed_in, down_share, up_terms = tie((grad_feed_in, down_share, up_terms))

    grad_resid = grad_out + grad_feed_in
    grad_branch, grad_attention_gain = norm_back(branch_attn, attn_factor, gains[0], grad_resid)
    gathered = gather_plane(grad_branch.astype(BF))
    grad_branch_all = jnp.concatenate(gathered[0] + gathered[1], 0)
    grad_mixed = contract_cols(grad_branch_all, out_block).astype(BF)
    grad_mixed = plane_absolute(grad_mixed.reshape(parts, rows, head_cols))
    grad_mixed = lax.all_to_all(
        grad_mixed.reshape(shards, 2 * rows, head_cols), "z", 0, 0, tiled=True
    ).reshape(seq_len, head_cols)
    grad_output = contract_rows(attended, grad_branch_all).astype(BF)
    output_rows = head_cols // planes
    output_part = grad_output.reshape(planes, output_rows, width // head_cols, head_cols).transpose(0, 2, 1, 3)
    output_part, grad_mixed, gate_share = tie((output_part, grad_mixed, gate_share))
    down_all = copies(down_share)
    scaled_q, scaled_k, grad_values, inner, grad_gains = attend_backward(
        query_low, key_low, value_low, grad_mixed, attended_seq, raw, squares, query_gain_here, key_gain_here,
        cosine, sine, key_bias, block_flags, lse, per_block,
    )
    inner, up_share, down_share = tie((inner, up_share, down_share))
    inner = sum_plane(jnp.sum(inner, 0).reshape(2, 2, seq_len // 2), True).reshape(squares.shape)
    grad_raw = finish(scaled_q, scaled_k, grad_values, raw, squares, inner)
    input_part = input_terms(inputs_here, grad_raw, planes)
    heads_part = jnp.concatenate(
        [input_part.reshape(planes, -1, head_cols), output_part.reshape(planes, -1, head_cols)], 1
    )
    grad_raw, heads_part = tie((grad_raw, heads_part))
    heads_part, down_all = tie((heads_part, down_all))
    heads_share = plane_share(heads_part)
    share = chunk // planes
    input_share = heads_share[: shards * 3 * share].reshape(shards, 3 * share, head_cols)
    output_share = heads_share[shards * 3 * share :]
    seq_half = seq_len // 2

    def chunks_of(values):
        return jnp.stack([contract_cols(values, block[:chunk]) for block in input_blocks]).astype(BF)

    grad_chunk, _ = reduce_plane(chunks_of(grad_raw[seq_half:]), chunks_of(grad_raw[:seq_half]), ())
    grad_chunk = grad_chunk.astype(BF).reshape(planes, rows, chunk)
    grad_chunk = jnp.stack([send_plane(grad_chunk[k], k) if k else grad_chunk[k] for k in range(planes)])
    by_shard = [
        lax.dynamic_index_in_dim(grad_chunk, shard ^ plane ^ k, 0, keepdims=False) for k in range(shards)
    ]
    by_shard = [send_shard(by_shard[k], k) if k else by_shard[k] for k in range(shards)]
    grad_chunk = absolute_shards(by_shard)
    grad_tokens = grad_resid + grad_chunk.transpose(1, 0, 2).reshape(rows, width).astype(F32)

    grad_down_weight = rows_out(down_all)
    (grad_gate_weight,) = columns_out(copies(to_owner(gate_share, False)), 1)
    (grad_up_weight,) = columns_out(copies(to_owner(up_share, False)), 1)
    input_share = to_owner(input_share, True).reshape(-1, head_cols)
    heads_all = copies(jnp.concatenate([input_share, output_share], 0))
    grad_query_weight, grad_key_weight, grad_value_weight, grad_output_weight = attention_out(heads_all, shards, share)
    grad_output_weight = grad_output_weight.reshape(output_weight.shape)

    valid = (pad_flags[0] == 0).astype(F32)[:, None]
    stat_terms = jnp.stack(
        [
            jnp.sum(valid * result * result),
            jnp.sum(valid * branch_attn * branch_attn),
            jnp.sum(valid * branch_feed * branch_feed),
            jnp.sum(valid),
        ]
    )
    terms = jnp.concatenate([grad_attention_gain, grad_feed_gain, jnp.pad(stat_terms, (0, 124))])
    terms = sum_over_planes(sum_plane(terms.reshape(-1, 128))).reshape(-1)
    gain_width = query_gain.shape[0]
    gain_full = terms[: 2 * width].reshape(2, width)
    gain_full = lax.dynamic_slice_in_dim(gain_full, shard * gain_width, gain_width, 1)
    stat_terms = terms[2 * width :]
    stats = jnp.sqrt(stat_terms[:3] / (stat_terms[3] * width))
    gain_heads = sum_over_planes(grad_gains.transpose(1, 0, 2).reshape(2, head_cols))
    gain_other = send_core(gain_heads)
    gain_heads = jnp.where(
        core == 0,
        jnp.concatenate([gain_heads, gain_other], 1),
        jnp.concatenate([gain_other, gain_heads], 1),
    )
    return (
        result[None],
        grad_tokens[None],
        grad_query_weight,
        grad_key_weight,
        grad_value_weight,
        grad_output_weight,
        grad_gate_weight,
        grad_up_weight,
        grad_down_weight,
        gain_heads[0],
        gain_heads[1],
        gain_full[0],
        gain_full[1],
        stats,
    )


def solution(mesh):
    devices = mesh.devices.reshape(mesh.shape["replica"] // 2, 2, mesh.shape["shard"])
    split = Mesh(devices, ("z", "core", "shard"))
    tokens = ("z", "core")
    placed = (
        (P("shard", tokens, None), P("shard", tokens), P("shard", tokens), P("shard", tokens, None))
        + (P("shard", None),) * 7
        + (P("shard"),) * 4
    )
    return jax.shard_map(
        per_device,
        mesh=split,
        in_specs=placed,
        out_specs=(P("shard", tokens, None),) * 2
        + (P("shard", None),) * 7
        + (P("shard"),) * 4
        + (P(),),
        check_vma=False,
    )
```

```python
import functools

import jax
import jax.numpy as jnp
from jax import lax
from jax.experimental import pallas as pl
from jax.experimental.pallas import tpu as pltpu
from jax.sharding import Mesh, PartitionSpec as P

HEADS = 16
HEAD = 128
PIECE = 256

epsilon = 1e-06
theta_base = 500000.0
masked_score = -1e30
score_scale = HEAD ** (-0.5)

BF = jnp.bfloat16
F32 = jnp.float32


def mm(left, right):
    return jnp.dot(left, right, preferred_element_type=F32)


def contract_rows(left, right):
    return lax.dot_general(left, right, (((0,), (0,)), ((), ())), preferred_element_type=F32)


def contract_cols(left, right):
    return lax.dot_general(left, right, (((1,), (1,)), ((), ())), preferred_element_type=F32)


def send_core(values):
    return lax.ppermute(values, "core", [(0, 1), (1, 0)])


def send_shard(values, k):
    count = lax.axis_size("shard")
    return lax.ppermute(values, "shard", [(i, i ^ k) for i in range(count)])


def send_plane(values, k):
    count = lax.axis_size("z")
    return lax.ppermute(values, "z", [(i, i ^ k) for i in range(count)])


def gather_shard(values):
    count = lax.axis_size("shard")
    if count != 4:
        return [values] + [send_shard(values, k) for k in range(1, count)]
    half = values.shape[0] // 2
    from_x = send_shard(values, 1)
    from_y = send_shard(values, 2)
    far_a = send_shard(from_x[:half], 2)
    far_b = send_shard(from_y[half:], 1)
    return [values, from_x, from_y, jnp.concatenate([far_a, far_b], 0)]


def gather_plane(values):
    mine = gather_shard(values)
    return [mine, [send_core(block) for block in mine]]


def reduce_steps(term):
    count = lax.axis_size("shard")
    everything = slice(None)
    if count != 4:
        got = yield [send_shard(term(k, everything).astype(BF), k) for k in range(1, count)]
        result = term(0, everything)
        for values in got:
            result = result + values.astype(F32)
        return result
    near, far = slice(0, term.rows // 2), slice(term.rows // 2, None)
    via_x, via_y = yield (send_shard(term(3, near).astype(BF), 1), send_shard(term(3, far).astype(BF), 2))
    to_y = jnp.concatenate([(term(2, near) + via_x.astype(F32)).astype(BF), term(2, far).astype(BF)], 0)
    to_x = jnp.concatenate([term(1, near).astype(BF), (term(1, far) + via_y.astype(F32)).astype(BF)], 0)
    from_x, from_y = yield (send_shard(to_x, 1), send_shard(to_y, 2))
    return term(0, everything) + from_x.astype(F32) + from_y.astype(F32)


def run_steps(steps, between=lambda values: values):
    values = next(steps)
    while True:
        try:
            values = steps.send(between(values))
        except StopIteration as stop:
            return stop.value


def reduce_shard(term):
    return run_steps(reduce_steps(term))


def reduce_plane(other, mine, also):
    got = send_core(other.astype(BF))
    mine, got, also = lax.optimization_barrier((mine.astype(BF), got, also))

    def term(k, part):
        return mine[k, part].astype(F32) + got[k, part].astype(F32)

    term.rows = mine.shape[1]
    return reduce_shard(term), also


def sum_over_planes(values):
    parts = [send_plane(values, k) for k in range(1, lax.axis_size("z"))]
    return sum(parts, values)


def sum_plane(values, swapped=False):
    count = lax.axis_size("shard")
    other = send_core(values)
    values = values + (other[:, ::-1] if swapped else other)
    step = 1
    while step < count:
        values = values + send_shard(values, step)
        step *= 2
    return values


def terms_kernel(tokens, grads, out):
    total = contract_rows(tokens[...], grads[...]).astype(BF)
    out[...] = total.reshape(out.shape)


def weight_terms(tokens, grads, shards, planes):
    rows, width = tokens.shape
    cols = grads.shape[1]
    chunk = width // shards
    return pl.pallas_call(
        terms_kernel,
        grid=(shards,),
        in_specs=[
            pl.BlockSpec((rows, chunk), lambda i: (0, i)),
            pl.BlockSpec((rows, cols), lambda i: (0, 0), pipeline_mode=pl.Buffered(1)),
        ],
        out_specs=pl.BlockSpec((planes, 1, chunk // planes, cols), lambda i: (0, i, 0, 0)),
        out_shape=jax.ShapeDtypeStruct((planes, shards, chunk // planes, cols), BF),
        compiler_params=pltpu.CompilerParams(vmem_limit_bytes=40 * 1024 * 1024),
        name="weight_terms",
    )(tokens, grads)


def columns_kernel(copies, *outs):
    _, cores, shards, rows, cols = copies.shape
    share = cols // len(outs)
    for n, out in enumerate(outs):
        for s in range(shards):
            for c in range(cores):
                at = (s * cores + c) * share
                out[:, at : at + share] = copies[0, c, s, :, n * share : (n + 1) * share].astype(F32)


def columns_out(copies, count):
    planes, cores, shards, rows, cols = copies.shape
    wide = shards * cores * cols // count
    return pl.pallas_call(
        columns_kernel,
        grid=(planes,),
        in_specs=[pl.BlockSpec((1,) + copies.shape[1:], lambda i: (i, 0, 0, 0, 0))],
        out_specs=[pl.BlockSpec((rows, wide), lambda i: (i, 0))] * count,
        out_shape=[jax.ShapeDtypeStruct((planes * rows, wide), F32)] * count,
        compiler_params=pltpu.CompilerParams(vmem_limit_bytes=40 * 1024 * 1024),
        name="columns_out",
    )(copies)


def rows_kernel(copies, out):
    out[...] = copies[0, 0].astype(F32)


def rows_out(copies):
    planes, cores, rows, cols = copies.shape
    return pl.pallas_call(
        rows_kernel,
        grid=(planes, cores),
        in_specs=[pl.BlockSpec((1, 1, rows, cols), lambda i, j: (i, j, 0, 0))],
        out_specs=pl.BlockSpec((rows, cols), lambda i, j: (j * planes + i, 0)),
        out_shape=jax.ShapeDtypeStruct((planes * cores * rows, cols), F32),
        name="rows_out",
    )(copies)


def project_kernel(count, *refs):
    tokens, weights, raw, squares = refs[: 2 * count], refs[2 * count : 3 * count], refs[-2], refs[-1]
    chunk = tokens[0].shape[1]
    third = raw.shape[1] // 3
    block = pl.program_id(0) * pl.num_programs(1) + pl.program_id(1)
    for r in range(2):

        @pl.when(pl.program_id(0) == r)
        def _():
            total = mm(tokens[r * count][...], weights[0][:chunk, :])
            for k in range(1, count):
                total += mm(tokens[r * count + k][...], weights[k][:chunk, :])
            raw[...] = total
            for n in range(2):
                squared = total[:, n * third : (n + 1) * third]
                squared = squared * squared
                folded = squared[:, :HEAD]
                for h in range(1, third // HEAD):
                    folded += squared[:, h * HEAD : (h + 1) * HEAD]
                squares[n, pl.ds(block, 1), :] = as_row(folded)


def project(pieces, weights):
    count = len(weights)
    rows, chunk = pieces[0][0].shape
    cols = weights[0].shape[1]
    steps = rows // PIECE

    def spec(r):
        return pl.BlockSpec((PIECE, chunk), lambda a, i: (jnp.where(a == r, i, (steps - 1) * (a > r)), 0))

    return pl.pallas_call(
        functools.partial(project_kernel, count),
        grid=(2, steps),
        in_specs=[spec(r) for r in range(2) for _ in range(count)]
        + [pl.BlockSpec(w.shape, lambda a, i: (0, 0), pipeline_mode=pl.Buffered(1)) for w in weights],
        out_specs=[
            pl.BlockSpec((PIECE, cols), lambda a, i: (a * steps + i, 0)),
            pl.BlockSpec((2, 2 * steps, PIECE), lambda a, i: (0, 0, 0)),
        ],
        out_shape=[
            jax.ShapeDtypeStruct((2 * rows, cols), F32),
            jax.ShapeDtypeStruct((2, 2 * steps, PIECE), F32),
        ],
        compiler_params=pltpu.CompilerParams(vmem_limit_bytes=40 * 1024 * 1024),
        name="project",
    )(*pieces[0], *pieces[1], *weights)


def input_terms_kernel(count, *refs):
    tokens, grads, out = refs[: 2 * count], refs[2 * count], refs[2 * count + 1]
    rows = tokens[0].shape[0]
    planes, _, _, share, third = out.shape
    for k in range(count):
        total = contract_rows(tokens[k][...], grads[:rows, :]) + contract_rows(tokens[count + k][...], grads[rows:, :])
        for n in range(3):
            out[:, k, n] = total[:, n * third : (n + 1) * third].astype(BF).reshape(planes, share, third)


def input_terms(pieces, grads, planes):
    count = len(pieces[0])
    chunk = pieces[0][0].shape[1]
    return pl.pallas_call(
        functools.partial(input_terms_kernel, count),
        out_shape=jax.ShapeDtypeStruct((planes, count, 3, chunk // planes, grads.shape[1] // 3), BF),
        compiler_params=pltpu.CompilerParams(vmem_limit_bytes=56 * 1024 * 1024),
        name="input_terms",
    )(*pieces[0], *pieces[1], grads)


def attention_out_kernel(shards, share, copies, query, key, value, output):
    _, cores, _, cols = copies.shape
    for n, out in enumerate((query, key, value)):
        for s in range(shards):
            for c in range(cores):
                at = (s * cores + c) * cols
                row = (s * 3 + n) * share
                out[:, at : at + cols] = copies[0, c, row : row + share, :].astype(F32)
    first = shards * 3 * share
    rows = output.shape[1]
    for c in range(cores):
        for j in range(output.shape[2] // cols):
            row = first + j * rows
            output[c, :, j * cols : (j + 1) * cols] = copies[0, c, row : row + rows, :].astype(F32)


def attention_out(copies, shards, share):
    planes, cores, total, cols = copies.shape
    wide = shards * cores * cols
    rows = (total - shards * 3 * share) * cols // wide
    return pl.pallas_call(
        functools.partial(attention_out_kernel, shards, share),
        grid=(planes,),
        in_specs=[pl.BlockSpec((1, cores, total, cols), lambda i: (i, 0, 0, 0))],
        out_specs=[pl.BlockSpec((share, wide), lambda i: (i, 0))] * 3
        + [pl.BlockSpec((cores, rows, wide), lambda i: (0, i, 0))],
        out_shape=[jax.ShapeDtypeStruct((planes * share, wide), F32)] * 3
        + [jax.ShapeDtypeStruct((cores, planes * rows, wide), F32)],
        compiler_params=pltpu.CompilerParams(vmem_limit_bytes=40 * 1024 * 1024),
        name="attention_out",
    )(copies)


def memory_block(block, where, blocks, per_device):
    core, here = where
    plane, rest = divmod(block, 2 * per_device)
    which, inside = divmod(rest, per_device)
    return (which ^ core) * (blocks // 2) + (plane ^ here) * per_device + inside


def as_columns(row):
    return jnp.broadcast_to(row, (HEAD, PIECE)).T


def as_row(values):
    return jnp.sum(values.T, axis=0, keepdims=True)


def factor_of(squares):
    return lax.rsqrt(squares * (1.0 / (HEADS * HEAD)) + epsilon)


def forward_kernel(
    per_device, flags, raw_q, raw_k, raw_v, squares, gain_q, gain_k, cosine, sine, key_bias,
    mixed, queries, keys, values, lse,
):
    rows = queries.shape[0]
    blocks = rows // PIECE
    core = (flags[blocks], flags[blocks + 1])
    place_key = lax.broadcasted_iota(jnp.int32, (PIECE, PIECE), 0)
    place_query = lax.broadcasted_iota(jnp.int32, (PIECE, PIECE), 1)
    causal = place_key <= place_query
    for b in range(blocks):
        here = pl.ds(b * PIECE, PIECE)
        from_block = memory_block(b, core, blocks, per_device)
        there = pl.ds(pl.multiple_of(from_block * PIECE, PIECE), PIECE)
        for n, (raw, gain, turned) in enumerate(((raw_q, gain_q, queries), (raw_k, gain_k, keys))):
            factor = as_columns(factor_of(squares[n, pl.ds(from_block, 1), :]))
            normed = raw[there, :] * factor * gain[...]
            turned[here, :] = (
                normed * cosine[here, :] + pltpu.roll(normed, HEAD // 2, 1) * sine[here, :]
            ).astype(BF)
        values[here, :] = raw_v[there, :].astype(BF)
    for b in range(blocks):
        here = pl.ds(b * PIECE, PIECE)
        seen = pl.ds(0, (b + 1) * PIECE)
        whole = flags[b] > 0
        scores = contract_cols(keys[seen, :], queries[here, :]) * score_scale + key_bias[seen, :]
        last = jnp.where(causal | whole, scores[b * PIECE :], masked_score)
        scores = jnp.concatenate([scores[: b * PIECE], last], 0) if b else last
        highest = jnp.max(scores, axis=0, keepdims=True)
        raised = jnp.exp(scores - highest)
        summed = jnp.sum(raised, axis=0, keepdims=True)
        lse[:, here] = highest + jnp.log(summed)
        probs = (raised * (1.0 / summed)).astype(BF)
        mixed[here, :] = contract_rows(probs, values[seen, :]).astype(mixed.dtype)


def attend_forward(raw, squares, gain_q, gain_k, cosine, sine, key_bias, flags, per_device):
    rows = raw.shape[0]
    heads = raw.shape[1] // (3 * HEAD)
    blocks = rows // PIECE
    column = pl.BlockSpec((rows, HEAD), lambda h, f: (0, h))
    table = pl.BlockSpec((rows, HEAD), lambda h, f: (0, 0), pipeline_mode=pl.Buffered(1))
    gain = pl.BlockSpec((1, HEAD), lambda h, f: (0, h))
    turned = jax.ShapeDtypeStruct((rows, heads * HEAD), BF)
    return pl.pallas_call(
        functools.partial(forward_kernel, per_device),
        grid_spec=pltpu.PrefetchScalarGridSpec(
            num_scalar_prefetch=1,
            grid=(heads,),
            in_specs=[
                column,
                pl.BlockSpec((rows, HEAD), lambda h, f: (0, heads + h)),
                pl.BlockSpec((rows, HEAD), lambda h, f: (0, 2 * heads + h)),
                pl.BlockSpec((2, blocks, PIECE), lambda h, f: (0, 0, 0)),
                gain,
                gain,
                table,
                table,
                pl.BlockSpec((rows, 1), lambda h, f: (0, 0), pipeline_mode=pl.Buffered(1)),
            ],
            out_specs=[column] * 4 + [pl.BlockSpec((None, 1, rows), lambda h, f: (h, 0, 0))],
        ),
        out_shape=[turned] * 4 + [jax.ShapeDtypeStruct((heads, 1, rows), F32)],
        compiler_params=pltpu.CompilerParams(vmem_limit_bytes=52 * 1024 * 1024),
        name="attend_forward",
    )(flags, raw, raw, raw, squares, gain_q, gain_k, cosine, sine, key_bias)


def backward_kernel(
    per_device, flags, queries, keys, values, grad_mixed, mixed, raw_q, raw_k, squares, gain_q, gain_k,
    cosine, sine, key_bias, lse,
    scaled_q, scaled_k, grad_values, inner, grad_gains, keys_acc, values_acc,
):
    rows = queries.shape[0]
    blocks = rows // PIECE
    core = (flags[blocks], flags[blocks + 1])
    place_key = lax.broadcasted_iota(jnp.int32, (PIECE, PIECE), 0)
    place_query = lax.broadcasted_iota(jnp.int32, (PIECE, PIECE), 1)
    causal = place_key <= place_query
    keys_acc[...] = jnp.zeros_like(keys_acc)
    values_acc[...] = jnp.zeros_like(values_acc)
    grad_gains[...] = jnp.zeros_like(grad_gains)

    def turn_back(n, b, grad, raw, gain, scaled_out):
        here = pl.ds(b * PIECE, PIECE)
        block = memory_block(b, core, blocks, per_device)
        there = pl.ds(pl.multiple_of(block * PIECE, PIECE), PIECE)
        turned = grad * cosine[here, :] - pltpu.roll(grad, HEAD // 2, 1) * sine[here, :]
        raw_block = raw[there, :]
        scaled = turned * gain[...]
        scaled_out[there, :] = scaled
        inner[n, pl.ds(block, 1), :] = as_row(raw_block * scaled)
        factor = as_columns(factor_of(squares[n, pl.ds(block, 1), :]))
        grad_gains[n : n + 1, :] += jnp.sum(turned * raw_block * factor, axis=0, keepdims=True)

    for b in range(blocks):
        here = pl.ds(b * PIECE, PIECE)
        whole = flags[b] > 0
        query_block = queries[here, :]
        grad_block = grad_mixed[here, :]
        delta = as_row(grad_block.astype(F32) * mixed[here, :].astype(F32))
        grad_query = jnp.zeros((PIECE, HEAD), F32)
        for first in range(0, b + 1, 8):
            last = min(first + 8, b + 1)
            seen = pl.ds(first * PIECE, (last - first) * PIECE)
            scores = contract_cols(keys[seen, :], query_block) * score_scale + key_bias[seen, :]
            if last == b + 1:
                edge = (b - first) * PIECE
                final = jnp.where(causal | whole, scores[edge:], masked_score)
                scores = jnp.concatenate([scores[:edge], final], 0) if edge else final
            probs = jnp.exp(scores - lse[:, here])
            grad_probs = contract_cols(values[seen, :], grad_block)
            grad_scores = (probs * (grad_probs - delta)).astype(BF)
            values_acc[seen, :] += mm(probs.astype(BF), grad_block)
            keys_acc[seen, :] += mm(grad_scores, query_block)
            grad_query += contract_rows(grad_scores, keys[seen, :])
        turn_back(0, b, grad_query * score_scale, raw_q, gain_q, scaled_q)
    for b in range(blocks):
        here = pl.ds(b * PIECE, PIECE)
        turn_back(1, b, keys_acc[here, :] * score_scale, raw_k, gain_k, scaled_k)
        block = memory_block(b, core, blocks, per_device)
        there = pl.ds(pl.multiple_of(block * PIECE, PIECE), PIECE)
        grad_values[there, :] = values_acc[here, :].astype(BF)


def attend_backward(
    queries, keys, values, grad_mixed, mixed, raw, squares, gain_q, gain_k, cosine, sine, key_bias, flags, lse,
    per_device,
):
    rows, width = queries.shape
    heads = width // HEAD
    blocks = rows // PIECE
    column = pl.BlockSpec((rows, HEAD), lambda h, f: (0, h))
    table = pl.BlockSpec((rows, HEAD), lambda h, f: (0, 0), pipeline_mode=pl.Buffered(1))
    gain = pl.BlockSpec((1, HEAD), lambda h, f: (0, h))
    return pl.pallas_call(
        functools.partial(backward_kernel, per_device),
        grid_spec=pltpu.PrefetchScalarGridSpec(
            num_scalar_prefetch=1,
            grid=(heads,),
            in_specs=[column] * 5
            + [
                column,
                pl.BlockSpec((rows, HEAD), lambda h, f: (0, heads + h)),
                pl.BlockSpec((2, blocks, PIECE), lambda h, f: (0, 0, 0)),
                gain,
                gain,
                table,
                table,
                pl.BlockSpec((rows, 1), lambda h, f: (0, 0), pipeline_mode=pl.Buffered(1)),
                pl.BlockSpec((None, 1, rows), lambda h, f: (h, 0, 0)),
            ],
            out_specs=[column] * 3
            + [
                pl.BlockSpec((None, 2, blocks, PIECE), lambda h, f: (h, 0, 0, 0)),
                pl.BlockSpec((None, 2, HEAD), lambda h, f: (h, 0, 0)),
            ],
            scratch_shapes=[pltpu.VMEM((rows, HEAD), F32)] * 2,
        ),
        out_shape=[
            jax.ShapeDtypeStruct((rows, width), F32),
            jax.ShapeDtypeStruct((rows, width), F32),
            jax.ShapeDtypeStruct((rows, width), BF),
            jax.ShapeDtypeStruct((heads, 2, blocks, PIECE), F32),
            jax.ShapeDtypeStruct((heads, 2, HEAD), F32),
        ],
        compiler_params=pltpu.CompilerParams(vmem_limit_bytes=56 * 1024 * 1024),
        name="attend_backward",
    )(
        flags, queries, keys, values, grad_mixed, mixed, raw, raw, squares, gain_q, gain_k, cosine, sine,
        key_bias, lse,
    )


def finish_kernel(scaled_q, scaled_k, grad_values, raw, squares, inner, out):
    block = pl.program_id(0)
    width = scaled_q.shape[1]
    for n, scaled in enumerate((scaled_q, scaled_k)):
        factor_row = factor_of(squares[n, pl.ds(block, 1), :])
        inner_row = inner[n, pl.ds(block, 1), :] * (1.0 / (HEADS * HEAD))
        factor = as_columns(factor_row)
        slope = as_columns(factor_row * factor_row * factor_row * inner_row)
        for h in range(width // HEAD):
            at = n * width + h * HEAD
            out[:, at : at + HEAD] = (
                factor * scaled[:, h * HEAD : (h + 1) * HEAD] - raw[:, at : at + HEAD] * slope
            ).astype(BF)
    out[:, 2 * width :] = grad_values[...]


def finish(scaled_q, scaled_k, grad_values, raw, squares, inner):
    rows, width = scaled_q.shape
    blocks = rows // PIECE
    part = pl.BlockSpec((PIECE, width), lambda i: (i, 0))
    wide = pl.BlockSpec((PIECE, 3 * width), lambda i: (i, 0))
    row = pl.BlockSpec((2, blocks, PIECE), lambda i: (0, 0, 0))
    return pl.pallas_call(
        finish_kernel,
        grid=(blocks,),
        in_specs=[part, part, part, wide, row, row],
        out_specs=wide,
        out_shape=jax.ShapeDtypeStruct((rows, 3 * width), BF),
        name="finish",
    )(scaled_q, scaled_k, grad_values, raw, squares, inner)


def norm_factor(values):
    return lax.rsqrt(jnp.mean(values * values, axis=-1, keepdims=True) + epsilon)


def norm_back(values, factor, gain, cotangent):
    scaled = gain * cotangent
    inner = jnp.mean(values * scaled, axis=-1, keepdims=True)
    grad = factor * scaled - values * (factor * factor * factor) * inner
    return grad, jnp.sum(cotangent * values * factor, axis=0)


def per_device(
    hidden_in,
    piece_index,
    pad_flags,
    cotangent,
    query_weight,
    key_weight,
    value_weight,
    output_weight,
    gate_weight,
    up_weight,
    down_weight,
    query_gain,
    key_gain,
    attention_gain,
    feed_gain,
):
    shards = lax.axis_size("shard")
    planes = lax.axis_size("z")
    shard = lax.axis_index("shard")
    core = lax.axis_index("core")
    plane = lax.axis_index("z")
    tokens = hidden_in[0]
    rows, width = tokens.shape
    chunk = width // shards
    parts = 2 * shards
    head_cols = width // parts
    feed_cols = gate_weight.shape[1] // parts
    seq_len = rows * 2 * planes
    everything = 2 * rows * shards

    tie = lax.optimization_barrier

    def plane_relative(values):
        return jnp.stack(
            [
                lax.dynamic_index_in_dim(values, (shard ^ k) * 2 + (core ^ r), 0, keepdims=False)
                for r in range(2)
                for k in range(shards)
            ]
        )

    def plane_absolute(values):
        return jnp.stack(
            [
                lax.dynamic_index_in_dim(values, (core ^ r) * shards + (shard ^ j), 0, keepdims=False)
                for j in range(shards)
                for r in range(2)
            ]
        )

    def absolute_shards(blocks):
        stacked = jnp.stack(blocks)
        return jnp.stack(
            [lax.dynamic_index_in_dim(stacked, shard ^ j, 0, keepdims=False) for j in range(shards)]
        )

    def column_block(weight, k, cols):
        return lax.dynamic_slice_in_dim(weight, ((shard ^ k) * 2 + core) * cols, cols, 1)

    gain_rows = jnp.pad(
        jnp.stack([attention_gain, feed_gain]), ((0, 14), (0, 3 * head_cols - attention_gain.shape[0]))
    )

    def input_block(k):
        block = [column_block(w, k, head_cols) for w in (query_weight, key_weight, value_weight)]
        return jnp.concatenate([jnp.concatenate(block, 1), gain_rows], 0)

    input_blocks = [input_block(0)] + [send_shard(input_block(k), k) for k in range(1, shards)]
    info_rows = 2 * rows // chunk
    info = jnp.stack([piece_index[0], pad_flags[0]]).astype(BF).reshape(info_rows, chunk)
    info = jnp.pad(info, ((0, 16 - info_rows), (0, 0)))

    def chunk_of(k):
        return jnp.concatenate([lax.dynamic_slice_in_dim(tokens, (shard ^ k) * chunk, chunk, 1), info], 0)

    by_seq = jnp.stack([send_shard(chunk_of(k), k) if k else chunk_of(k) for k in range(shards)])
    by_plane = [
        lax.dynamic_index_in_dim(by_seq, shard ^ plane ^ k, 0, keepdims=False) for k in range(planes)
    ]
    by_plane = jnp.stack([send_plane(by_plane[k], k) if k else by_plane[k] for k in range(planes)])
    rates = theta_base ** (-jnp.arange(HEAD // 2).astype(F32) * (2.0 / HEAD))
    angles = jnp.arange(seq_len, dtype=jnp.int32).astype(F32)[:, None] * rates[None, :]
    cosine, sine = jnp.cos(angles), jnp.sin(angles)
    cosine = jnp.concatenate([cosine, cosine], 1)
    sine = jnp.concatenate([-sine, sine], 1)
    by_plane, input_blocks, cosine, sine = tie((by_plane, input_blocks, cosine, sine))
    mine = by_plane[:, :rows].reshape(planes * rows, chunk)
    info_mine = by_plane[:, rows : rows + info_rows].reshape(planes, 2, rows)
    info_mine = jnp.stack(
        [lax.dynamic_index_in_dim(info_mine, plane ^ j, 0, keepdims=False) for j in range(planes)]
    )
    info_both = jnp.stack([info_mine, send_core(info_mine)], 1)
    info_seq = jnp.where(core == 0, info_both, info_both[:, ::-1]).astype(F32)
    piece_seq = info_seq[:, :, 0].reshape(seq_len)
    pad_seq = info_seq[:, :, 1].reshape(seq_len)
    block_flags = (piece_seq.reshape(-1, PIECE)[:, 0] >= 0.0).astype(jnp.int32)
    block_flags = jnp.concatenate([block_flags, core[None], plane[None]])
    key_bias = jnp.where(pad_seq > 0.0, masked_score, 0.0)[:, None]

    gains = absolute_shards([b[chunk : chunk + 2, : attention_gain.shape[0]] for b in input_blocks])
    gains = gains.transpose(1, 0, 2).reshape(2, width).astype(F32)
    out_block = lax.dynamic_slice_in_dim(output_weight, core * head_cols, head_cols, 0)
    down_block = lax.dynamic_slice_in_dim(down_weight, core * feed_cols, feed_cols, 0)
    query_gain_here = lax.dynamic_slice_in_dim(query_gain, core * head_cols, head_cols, 0).astype(F32)[None]
    key_gain_here = lax.dynamic_slice_in_dim(key_gain, core * head_cols, head_cols, 0).astype(F32)[None]

    def feed_block(k):
        return [column_block(w, k, feed_cols) for w in (gate_weight, up_weight)]

    last = shards - 1
    feed_own = [jnp.concatenate(feed_block(k), 1) for k in range(last)]
    feed_last = feed_block(last)
    gathered = gather_shard(mine)
    feed_own, feed_last, gathered = tie((feed_own, feed_last, gathered))
    gathered = [gathered, [send_core(block) for block in gathered]]
    gate_last = send_shard(feed_last[0], last)

    inputs_here = gathered
    raw, squares = project(inputs_here, input_blocks)
    squares = sum_plane(squares.reshape(2, 2, seq_len // 2), True)
    squares, gate_last, feed_own, feed_last = tie((squares, gate_last, feed_own, feed_last))
    feed_blocks = feed_own[:1] + [send_shard(feed_own[k], k) for k in range(1, last)]
    up_last = send_shard(feed_last[1], last)
    squares = squares.reshape(2, seq_len // PIECE, PIECE)
    per_block = rows // PIECE
    attended_seq, query_low, key_low, value_low, lse = attend_forward(
        raw, squares, query_gain_here, key_gain_here, cosine, sine, key_bias, block_flags, per_block
    )

    attended = lax.all_to_all(
        attended_seq.reshape(planes, 2 * rows, head_cols), "z", 0, 0, tiled=True
    ).reshape(parts, rows, head_cols)
    attended, feed_blocks = tie((attended, feed_blocks))
    attended = plane_relative(attended).reshape(everything, head_cols)
    half = everything // 2

    def blocks_of(values):
        return values.reshape(shards, rows, values.shape[-1])

    branch_attn, _ = reduce_plane(
        blocks_of(mm(attended[half:], out_block)), blocks_of(mm(attended[:half], out_block)), ()
    )
    branch_attn, up_last = tie((branch_attn, up_last))
    feed_blocks.append(jnp.concatenate([gate_last, up_last], 1))
    whole_feed = jnp.zeros((width, 2 * feed_cols), BF)
    for k in range(shards):
        whole_feed = lax.dynamic_update_slice_in_dim(whole_feed, feed_blocks[k], (shard ^ k) * chunk, 0)
    attn_factor = norm_factor(branch_attn)
    residual = tokens.astype(F32) + branch_attn * attn_factor * gains[0]
    gathered = gather_plane(residual.astype(BF))
    residual_all = jnp.concatenate(gathered[0] + gathered[1], 0)
    gate = mm(residual_all, whole_feed[:, :feed_cols])
    up = mm(residual_all, whole_feed[:, feed_cols:])
    activated = (jax.nn.silu(gate) * up).astype(BF)
    branch_feed, _ = reduce_plane(
        blocks_of(mm(activated[half:], down_block)), blocks_of(mm(activated[:half], down_block)), ()
    )
    feed_factor = norm_factor(branch_feed)
    result = residual + branch_feed * feed_factor * gains[1]

    grad_out = cotangent[0].astype(F32)
    grad_feed, grad_feed_gain = norm_back(branch_feed, feed_factor, gains[1], grad_out)
    gathered = gather_plane(grad_feed.astype(BF))
    grad_feed_all = jnp.concatenate(gathered[0] + gathered[1], 0)
    grad_down = contract_rows(activated, grad_feed_all).astype(BF)
    grad_down, grad_feed_all = tie((grad_down, grad_feed_all))

    def plane_share(terms):
        flat = terms.reshape(-1, terms.shape[-1])
        share = lax.psum_scatter(flat, "z", scatter_dimension=0, tiled=True)
        return share.reshape((1,) + terms.shape[1:])[0]

    def to_owner(share, relative):
        blocks = []
        for k in range(shards):
            block = share[k] if relative else lax.dynamic_index_in_dim(share, shard ^ k, 0, keepdims=False)
            blocks.append(send_shard(block, k) if k else block)
        return absolute_shards(blocks)

    def copies(values):
        whole = lax.all_gather(values, ("z", "core"), axis=0)
        return whole.reshape((planes, 2) + values.shape)

    down_share = plane_share(grad_down.reshape(planes, feed_cols // planes, width))
    grad_act = contract_cols(grad_feed_all, down_block)
    sigmoid = jax.nn.sigmoid(gate)
    grad_gate = (grad_act * up * sigmoid * (1.0 + gate * (1.0 - sigmoid))).astype(BF)
    grad_up = (grad_act * gate * sigmoid).astype(BF)

    def feed_back(part):
        return contract_cols(grad_gate[part], whole_feed[:, :feed_cols]) + contract_cols(
            grad_up[part], whole_feed[:, feed_cols:]
        )

    got_core = send_core(feed_back(slice(half, None)).astype(BF))
    gate_terms = weight_terms(residual_all, grad_gate, shards, planes)
    gate_terms, grad_gate, grad_up, got_core = tie((gate_terms, grad_gate, grad_up, got_core))
    gate_share = plane_share(gate_terms)
    to_mine = feed_back(slice(None, half)).astype(BF)
    to_mine, got_core, grad_up = tie((to_mine, got_core, grad_up))
    up_terms = weight_terms(residual_all, grad_up, shards, planes)
    up_share = plane_share(up_terms)

    def feed_term(k, part):
        return blocks_of(to_mine)[k, part].astype(F32) + blocks_of(got_core)[k, part].astype(F32)

    feed_term.rows = rows
    grad_feed_in = reduce_shard(feed_term)
    grad_feed_in, down_share, up_terms = tie((grad_feed_in, down_share, up_terms))

    grad_resid = grad_out + grad_feed_in
    grad_branch, grad_attention_gain = norm_back(branch_attn, attn_factor, gains[0], grad_resid)
    gathered = gather_plane(grad_branch.astype(BF))
    grad_branch_all = jnp.concatenate(gathered[0] + gathered[1], 0)
    grad_mixed = contract_cols(grad_branch_all, out_block).astype(BF)
    grad_mixed = plane_absolute(grad_mixed.reshape(parts, rows, head_cols))
    grad_mixed = lax.all_to_all(
        grad_mixed.reshape(shards, 2 * rows, head_cols), "z", 0, 0, tiled=True
    ).reshape(seq_len, head_cols)
    grad_output = contract_rows(attended, grad_branch_all).astype(BF)
    output_rows = head_cols // planes
    output_part = grad_output.reshape(planes, output_rows, width // head_cols, head_cols).transpose(0, 2, 1, 3)
    output_part, grad_mixed, gate_share = tie((output_part, grad_mixed, gate_share))
    down_all = copies(down_share)
    scaled_q, scaled_k, grad_values, inner, grad_gains = attend_backward(
        query_low, key_low, value_low, grad_mixed, attended_seq, raw, squares, query_gain_here, key_gain_here,
        cosine, sine, key_bias, block_flags, lse, per_block,
    )
    inner, up_share, down_share = tie((inner, up_share, down_share))
    inner = sum_plane(jnp.sum(inner, 0).reshape(2, 2, seq_len // 2), True).reshape(squares.shape)
    grad_raw = finish(scaled_q, scaled_k, grad_values, raw, squares, inner)
    input_part = input_terms(inputs_here, grad_raw, planes)
    heads_part = jnp.concatenate(
        [input_part.reshape(planes, -1, head_cols), output_part.reshape(planes, -1, head_cols)], 1
    )
    grad_raw, heads_part = tie((grad_raw, heads_part))
    heads_part, down_all = tie((heads_part, down_all))
    heads_share = plane_share(heads_part)
    share = chunk // planes
    input_share = heads_share[: shards * 3 * share].reshape(shards, 3 * share, head_cols)
    output_share = heads_share[shards * 3 * share :]
    seq_half = seq_len // 2

    def chunks_of(values):
        return jnp.stack([contract_cols(values, block[:chunk]) for block in input_blocks]).astype(BF)

    grad_chunk, _ = reduce_plane(chunks_of(grad_raw[seq_half:]), chunks_of(grad_raw[:seq_half]), ())
    grad_chunk = grad_chunk.astype(BF).reshape(planes, rows, chunk)
    grad_chunk = jnp.stack([send_plane(grad_chunk[k], k) if k else grad_chunk[k] for k in range(planes)])
    by_shard = [
        lax.dynamic_index_in_dim(grad_chunk, shard ^ plane ^ k, 0, keepdims=False) for k in range(shards)
    ]
    by_shard = [send_shard(by_shard[k], k) if k else by_shard[k] for k in range(shards)]
    grad_chunk = absolute_shards(by_shard)
    grad_tokens = grad_resid + grad_chunk.transpose(1, 0, 2).reshape(rows, width).astype(F32)

    grad_down_weight = rows_out(down_all)
    (grad_gate_weight,) = columns_out(copies(to_owner(gate_share, False)), 1)
    (grad_up_weight,) = columns_out(copies(to_owner(up_share, False)), 1)
    input_share = to_owner(input_share, True).reshape(-1, head_cols)
    heads_all = copies(jnp.concatenate([input_share, output_share], 0))
    grad_query_weight, grad_key_weight, grad_value_weight, grad_output_weight = attention_out(heads_all, shards, share)
    grad_output_weight = grad_output_weight.reshape(output_weight.shape)

    valid = (pad_flags[0] == 0).astype(F32)[:, None]
    stat_terms = jnp.stack(
        [
            jnp.sum(valid * result * result),
            jnp.sum(valid * branch_attn * branch_attn),
            jnp.sum(valid * branch_feed * branch_feed),
            jnp.sum(valid),
        ]
    )
    terms = jnp.concatenate([grad_attention_gain, grad_feed_gain, jnp.pad(stat_terms, (0, 124))])
    terms = sum_over_planes(sum_plane(terms.reshape(-1, 128))).reshape(-1)
    gain_width = query_gain.shape[0]
    gain_full = terms[: 2 * width].reshape(2, width)
    gain_full = lax.dynamic_slice_in_dim(gain_full, shard * gain_width, gain_width, 1)
    stat_terms = terms[2 * width :]
    stats = jnp.sqrt(stat_terms[:3] / (stat_terms[3] * width))
    gain_heads = sum_over_planes(grad_gains.transpose(1, 0, 2).reshape(2, head_cols))
    gain_other = send_core(gain_heads)
    gain_heads = jnp.where(
        core == 0,
        jnp.concatenate([gain_heads, gain_other], 1),
        jnp.concatenate([gain_other, gain_heads], 1),
    )
    return (
        result[None],
        grad_tokens[None],
        grad_query_weight,
        grad_key_weight,
        grad_value_weight,
        grad_output_weight,
        grad_gate_weight,
        grad_up_weight,
        grad_down_weight,
        gain_heads[0],
        gain_heads[1],
        gain_full[0],
        gain_full[1],
        stats,
    )


def solution(mesh):
    devices = mesh.devices.reshape(mesh.shape["replica"] // 2, 2, mesh.shape["shard"])
    split = Mesh(devices, ("z", "core", "shard"))
    tokens = ("z", "core")
    placed = (
        (P("shard", tokens, None), P("shard", tokens), P("shard", tokens), P("shard", tokens, None))
        + (P("shard", None),) * 7
        + (P("shard"),) * 4
    )
    return jax.shard_map(
        per_device,
        mesh=split,
        in_specs=placed,
        out_specs=(P("shard", tokens, None),) * 2
        + (P("shard", None),) * 7
        + (P("shard"),) * 4
        + (P(),),
        check_vma=False,
    )
```
